128 devices in a mesh: dp: 16 (over x_lo, z, core), loop: 8 (over x_hi, y).
Axes of the slice: x: 4 (x_hi: 2, x_lo: 2; x = x_hi * 2 + x_lo), y: 4, z: 4, core: 2. Of those that a mesh axis runs over, the one named last changes fastest.
Arguments:
- crop_tokens: bfloat16 [8192, 64, 1152], P(('dp', 'loop')), may hold values from -6 to 6
- crop_lengths: int32 [128, 64], P(('dp', 'loop')), may hold values from 1 to 64, 3072 in all within a row
- crop_owner: int32 [8192, 1], P(('dp', 'loop')), may hold values from 0 to 15; in each aligned block of 64 rows (0 to 63, 64 to 127, ...) at most 8 rows name the same one
- crop_slot: int32 [8192], P(('dp', 'loop')), may hold values from 0 to 31
- base_tokens: bfloat16 [4096, 32, 1152], P(('dp', 'loop')), may hold values from -1024 to 1024
- key_probe: bfloat16 [1152, 16], replicated, may hold values from -1 to 1
- value_weight: bfloat16 [1152, 1152], replicated, may hold values from -0.1875 to 0.1875
- out_weight: bfloat16 [1152, 1152], replicated, may hold values from -0.1875 to 0.1875
- text_embed: bfloat16 [4096, 1152], P(('dp', 'loop')), may hold values from -6 to 6
- pair_labels: int32 [4096], P(('dp', 'loop')), may hold values from 0 to 63
- logit_scale: float32 [1], replicated, may hold values from 2 to 8
- logit_bias: float32 [1], replicated, may hold values from -4 to -1
Outputs:
- image_embed: bfloat16 [4096, 1152], P(('dp', 'loop'))
- image_grad: float32 [4096, 1152], P(('dp', 'loop'))
- text_grad: float32 [4096, 1152], P(('dp', 'loop'))
The draws below stay inside these ranges and needn't reach their ends.
Inputs may be any that keep to these rules, and one draw needn't show every extreme that they name: `crop_owner`: at most 8 of the crops of one device name the same owner, and in every draw the crops of some device name one owner exactly 8 times. `crop_lengths`: the lengths of one device's crops sum to 3072 and the longest is exactly 64.
All inputs are finite; a program needn't handle non-finite values.
Results may differ from the reference program's by a relative error of at most 0.01.
Values may be sent and summed in bfloat16 or wider, within the bound.
No kernel may reach another device: no remote copies, remote signals or barrier semaphores. Data moves between devices by JAX's collectives and lax.ppermute only.
A program may use at most 192 MiB of HBM per device.

```python
import math
import jax
import jax.numpy as jnp
import numpy as np
from jax import lax

D = 1152
HEADS = 16
HEAD_DIM = 72
IMG_DEV = 32
CROP_TOK = 64
BASE_TOK = 32
CROPS_DEV = 64
CAP = 8
PAIRS = 4096
CROPS = 8192
GROUP = 256
N_DP = 16
N_LOOP = 8


def probe_draw(key):
    probe_key = jax.random.fold_in(key, 17)
    spread = math.sqrt(HEAD_DIM / D)
    limit = min(4.0, 1.0 / spread)
    return jax.random.truncated_normal(probe_key, -limit, limit, (D, HEADS), jnp.float32) * spread


def draw_key_probe(key, part):
    return probe_draw(key).astype(jnp.bfloat16)


def draw_base_tokens(key, part):
    noise_key = jax.random.fold_in(key, 23)
    return jax.random.truncated_normal(noise_key, -6.0, 6.0, (PAIRS, BASE_TOK, D), jnp.float32).astype(jnp.bfloat16)


def with_ends(drawn, stream_key, low, top_value):
    longest = drawn.shape.index(max(drawn.shape))
    spots = []
    for shift in (0, 1):
        where = [jax.random.randint(jax.random.fold_in(stream_key, axis), (), 0, length) for axis, length in enumerate(drawn.shape)]
        where[longest] = (where[longest] + shift) % drawn.shape[longest]
        spots.append(tuple(where))
    return drawn.at[spots[0]].set(low).at[spots[1]].set(top_value)


def level_of(stream_key, extent, split, low, largest):
    def one(dim, shards_of):
        steps = jax.random.uniform(jax.random.fold_in(jax.random.fold_in(stream_key, 6), dim), (shards_of,), jnp.float32, low / len(split), largest / len(split))
        return jnp.repeat(jnp.exp(steps), extent[dim] // shards_of).reshape((-1,) + (1,) * (len(extent) - dim - 1))

    loudness = one(*split[0])
    for cut in split[1:]:
        loudness = loudness * one(*cut)
    return loudness


def rank_table(amount, lean):
    portions = [(1 << 20) // math.isqrt(grade ** lean) + 1 for grade in range(1, amount + 1)]
    scale = 1 + sum(portions) // (1 << 30)
    return np.cumsum(np.array([max(1, weight // scale) for weight in portions]))


def ranked_ids(stream_key, extent, amount, lean):
    grid = rank_table(amount, lean)
    lot = jax.random.randint(jax.random.fold_in(stream_key, 1), extent, 0, int(grid[amount - 1]))
    standing = jnp.searchsorted(jnp.asarray(grid, jnp.int32), lot, side="right")
    return jax.random.permutation(jax.random.fold_in(stream_key, 2), amount)[standing].astype(jnp.int32)


def length_profile(count, total, bound, lean):
    portions = [(1 << 20) // math.isqrt(standing ** lean) + 1 for standing in range(2, count + 1)]
    surplus, counts = total - bound - (count - 1), [1] * (count - 1)
    while surplus > 0:
        free = [i for i in range(count - 1) if counts[i] < bound]
        mass, budget = sum([portions[i] for i in free]), surplus
        for i in free:
            addition = min(bound - counts[i], max(1, budget * portions[i] // mass), surplus)
            counts[i] = counts[i] + addition
            surplus = surplus - addition
    return np.array([bound] + counts)


def ragged(stream_key, count, total, most, slope):
    if count == 2:
        one = jax.random.randint(stream_key, (), max(1, total - most), min(most, total - 1) + 1)
        return jnp.stack([one, total - one])
    sizes = jnp.asarray(length_profile(count, total, most, slope), jnp.int32)
    pairs = (count - 1) // 2
    donor, sink = sizes[1:1 + 2 * pairs:2], sizes[2:2 + 2 * pairs:2]
    margin = jnp.minimum(donor - 1, most - sink)
    moved = jax.random.randint(jax.random.fold_in(stream_key, 1), (pairs,), 0, 1 << 20) % (margin + 1)
    sizes = sizes.at[1:1 + 2 * pairs:2].set(donor - moved).at[2:2 + 2 * pairs:2].set(sink + moved)
    return sizes[jax.random.permutation(jax.random.fold_in(stream_key, 2), count)]


def shared_out(key, own, number, rows, number_of, top, most, slope):
    order = jax.random.permutation(key, number_of)
    heavy_load, ordinary = portions_of(number_of, rows * top, most, slope, True), portions_of(number_of, rows * top, most, slope, False)
    places = jnp.arange(number_of)

    def named(sizes, rotation):
        used = int((sizes > 0).sum())
        fixed = max(1, used // 4)
        moved = fixed + (places - fixed + rotation * (used - fixed)) % max(1, number_of - fixed)
        return jnp.zeros((number_of,), jnp.int32).at[order[jnp.where(places < fixed, places, moved)]].set(jnp.asarray(sizes, jnp.int32))

    sizes = jnp.where(number % 4 == 0, named(heavy_load, number // 4), named(ordinary, number - number // 4 - 1))
    mixed = jax.random.permutation(jax.random.fold_in(own, 3), number_of)
    giver, receiver = mixed[0:number_of // 2 * 2:2], mixed[1:number_of // 2 * 2:2]
    room = jnp.minimum(sizes[giver] - 1, most - sizes[receiver]) // 2
    room = jnp.where((giver == order[0]) | (receiver == order[0]) | (sizes[receiver] == 0), 0, jnp.maximum(room, 0))
    moved = jax.random.randint(jax.random.fold_in(own, 4), (number_of // 2,), 0, 1 << 20) % (room + 1)
    sizes = sizes.at[giver].add(-moved).at[receiver].add(moved)
    items = jnp.searchsorted(jnp.cumsum(sizes), jnp.arange(rows * top), side="right").astype(jnp.int32)
    table = items.reshape(top, rows).T
    table = table[jax.random.permutation(jax.random.fold_in(own, 1), rows)]
    rotation = jax.random.randint(jax.random.fold_in(own, 2), (rows, 1), 0, top)
    return jnp.take_along_axis(table, (jnp.arange(top)[None, :] + rotation) % top, axis=1)


def portions_of(amount, total, most, skew, full):
    portions = [(1 << 20) // math.isqrt(rank ** skew) + 1 for rank in range(1, amount + 1)]
    largest = most if full else min(most, max(-(-total // amount), total * portions[0] // sum(portions)))
    least = 1 if total - largest >= amount - 1 else 0
    holding, surplus = [largest] + [least] * (amount - 1), total - largest - least * (amount - 1)
    while surplus > 0:
        free = [i for i in range(1, amount) if holding[i] < largest] or [i for i in range(1, amount) if holding[i] < most]
        mass, remaining = sum([portions[i] for i in free]), surplus
        for i in free:
            addition = min(most - holding[i], max(1, remaining * portions[i] // mass), surplus)
            holding[i] = holding[i] + addition
            surplus = surplus - addition
    return np.array(holding)


def noise(own_key, shape, scale, most, split=(), kind=jnp.bfloat16):
    gain = level_of(own_key, shape, split, -0.22, 0.18) if split else 1.0
    values = jax.random.normal(own_key, shape, jnp.float32) * scale * gain
    return jnp.minimum(jnp.maximum(values, -most), most).astype(kind)


def setup_inputs(seed: int = 0) -> dict:
    seeds = jax.random.split(jax.random.key(seed), 13)
    crop_tokens = noise(seeds[0], (CROPS, CROP_TOK, D), 1.0, 6.0, ((0, 128),))
    crop_lengths = jax.vmap(lambda own: ragged(own, CROPS_DEV, 3 * CROPS_DEV * CROP_TOK // 4, CROP_TOK, 2))(jax.random.split(seeds[1], (N_DP * N_LOOP))).reshape((N_DP * N_LOOP, CROPS_DEV)).astype(jnp.int32)
    crop_owner_keys = jax.random.split(jax.random.fold_in(seeds[2], 1), CROPS // CROPS_DEV)
    crop_owner_turns = jax.random.permutation(jax.random.fold_in(seeds[2], 3), CROPS // CROPS_DEV)
    crop_owner = jax.vmap(lambda own, number: shared_out(jax.random.fold_in(seeds[2], 2), own, number, CROPS_DEV, N_DP, 1, CAP, 2))(crop_owner_keys, crop_owner_turns).reshape((CROPS, 1))
    crop_slot = with_ends(jax.random.randint(seeds[3], (CROPS,), 0, IMG_DEV), jax.random.fold_in(seeds[3], 1), 0, IMG_DEV - 1).astype(jnp.int32)
    base_tokens = draw_base_tokens(jax.random.fold_in(seeds[12], 71), 0)
    key_probe = draw_key_probe(jax.random.fold_in(seeds[12], 71), 0)
    value_weight = noise(seeds[6], (D, D), D ** -0.5, 0.1875)
    out_weight = noise(seeds[7], (D, D), D ** -0.5, 0.1875)
    text_embed = noise(seeds[8], (PAIRS, D), 1.0, 6.0, ((0, 128),))
    pair_labels = with_ends(ranked_ids(seeds[9], (PAIRS,), GROUP // 4, 2), jax.random.fold_in(seeds[9], 3), 0, (GROUP // 4) - 1).astype(jnp.int32)
    logit_scale = jnp.clip(jnp.exp(jax.random.uniform(seeds[10], (1,), jnp.float32, math.log(2.0), math.log(8.0))), 2.0, 8.0)
    logit_bias = jnp.clip(jax.random.uniform(seeds[11], (1,), jnp.float32, -4.0, -1.0), -4.0, -1.0)
    return dict(crop_tokens=crop_tokens, crop_lengths=crop_lengths, crop_owner=crop_owner, crop_slot=crop_slot, base_tokens=base_tokens, key_probe=key_probe, value_weight=value_weight, out_weight=out_weight, text_embed=text_embed, pair_labels=pair_labels, logit_scale=logit_scale, logit_bias=logit_bias)


highest = lax.Precision.HIGHEST
norm_eps = 1e-06

def unit_rows(matrix):
    return matrix * lax.rsqrt(lax.optimization_barrier(jnp.sum(matrix * matrix, axis=1, keepdims=True)) + norm_eps)

def reference(crop_tokens, crop_lengths, crop_owner, crop_slot, base_tokens, key_probe, value_weight, out_weight, text_embed, pair_labels, logit_scale, logit_bias):
    crop_count = crop_tokens.shape[0]
    pair_count = base_tokens.shape[0]
    crop_index = jnp.arange(crop_count, dtype=jnp.int32)
    loop_pos = (crop_index // CROPS_DEV % N_LOOP).astype(jnp.int32)
    pair_of = ((crop_owner[:, 0] * N_LOOP + loop_pos) * IMG_DEV + crop_slot).astype(jnp.int32)
    lengths = crop_lengths.reshape(-1)
    crop_scores = jnp.dot(crop_tokens.reshape(-1, D), key_probe, preferred_element_type=jnp.float32)
    crop_scores = crop_scores.reshape(crop_count, CROP_TOK, HEADS) / math.sqrt(HEAD_DIM)
    position = jnp.arange(CROP_TOK, dtype=jnp.int32)
    is_valid = (position[None, :] < lengths[:, None])[:, :, None]
    crop_max = lax.optimization_barrier(jnp.max(jnp.where(is_valid, crop_scores, -jnp.inf), axis=1))
    base_scores = jnp.dot(base_tokens.reshape(-1, D), key_probe, preferred_element_type=jnp.float32)
    base_scores = base_scores.reshape(pair_count, BASE_TOK, HEADS) / math.sqrt(HEAD_DIM)
    joint_max = lax.optimization_barrier(jnp.max(base_scores, axis=1)).at[pair_of].max(crop_max)
    crop_weight = jnp.where(is_valid, jnp.exp(crop_scores - joint_max[pair_of][:, None, :]), 0.0)
    base_weight = jnp.exp(base_scores - joint_max[:, None, :])
    denominator = lax.optimization_barrier(jnp.sum(base_weight, axis=1)) + jax.ops.segment_sum(lax.optimization_barrier(jnp.sum(crop_weight, axis=1)), pair_of, num_segments=pair_count)
    value_heads = value_weight.astype(jnp.float32).reshape(D, HEADS, HEAD_DIM)

    def weighted_values(block_pair):
        tokens, weight = block_pair
        mixed_sum = jnp.einsum('ckh,ckd->chd', weight, tokens.astype(jnp.float32), precision=highest)
        projected = jnp.einsum('chd,dhe->che', mixed_sum, value_heads, precision=highest)
        return projected.reshape(tokens.shape[0], D)
    crop_parts = lax.map(weighted_values, (crop_tokens.reshape(-1, CROPS_DEV, CROP_TOK, D), crop_weight.reshape(-1, CROPS_DEV, CROP_TOK, HEADS))).reshape(crop_count, D)
    base_parts = lax.map(weighted_values, (base_tokens.reshape(-1, IMG_DEV, BASE_TOK, D), base_weight.reshape(-1, IMG_DEV, BASE_TOK, HEADS))).reshape(pair_count, D)
    summed = base_parts + jax.ops.segment_sum(crop_parts, pair_of, num_segments=pair_count)
    pooled = (summed.reshape(pair_count, HEADS, HEAD_DIM) / denominator[:, :, None]).reshape(pair_count, D).astype(jnp.bfloat16)
    features = jnp.dot(pooled, out_weight, preferred_element_type=jnp.float32)
    image_embed = features.astype(jnp.bfloat16)
    image_unit = unit_rows(features).astype(jnp.bfloat16)
    text_unit = unit_rows(text_embed.astype(jnp.float32)).astype(jnp.bfloat16)
    image_groups = image_unit.astype(jnp.float32).reshape(N_DP, GROUP, D)
    text_groups = text_unit.astype(jnp.float32).reshape(N_DP, GROUP, D)
    label_groups = pair_labels.reshape(N_DP, GROUP)
    scale_value = logit_scale[0]
    bias_value = logit_bias[0]
    logits = scale_value * jnp.einsum('gid,gjd->gij', image_groups, text_groups, precision=highest) + bias_value
    target_sign = jnp.where(label_groups[:, :, None] == label_groups[:, None, :], 1.0, -1.0)
    grad_tile = (scale_value * (-target_sign * jax.nn.sigmoid(-target_sign * logits))).astype(jnp.bfloat16)
    grad_tile = lax.optimization_barrier(grad_tile).astype(jnp.float32)
    image_grad = jnp.einsum('gij,gjd->gid', grad_tile, text_groups, precision=highest).reshape(pair_count, D)
    text_grad = jnp.einsum('gij,gid->gjd', grad_tile, image_groups, precision=highest).reshape(pair_count, D)
    return (image_embed, image_grad, text_grad)
```

```python
import math

import jax
import jax.numpy as jnp
from jax import lax
from jax.experimental import pallas as pl
from jax.experimental.pallas import tpu as pltpu
from jax.sharding import PartitionSpec as P

very_low = -1e30
norm_eps = 1e-06
highest = lax.Precision.HIGHEST
f32 = jnp.float32
bf16 = jnp.bfloat16
contract_last = (((1,), (1,)), ((), ()))
lanes = 128
col_tile = 256


def iota(shape, dim):
    return lax.broadcasted_iota(jnp.int32, shape, dim)


def column_tiles(width, head_dim):
    tiles = []
    for low in range(0, width, col_tile):
        high = min(low + col_tile, width)
        tiles.append((low, high, low // head_dim, (high - 1) // head_dim))
    return tiles


def own_head(shape, low, head, head_dim):
    column = iota(shape, 1) + low
    return (column >= head * head_dim) & (column < (head + 1) * head_dim)


def gather_heads(mixed_ref, rows_ref, count, heads):
    for part in range(rows_ref.shape[1] // lanes):
        for head in range(heads):
            rows_ref[head * count : (head + 1) * count, part * lanes : (part + 1) * lanes] = (
                mixed_ref[pl.ds(part * count * heads + head, count, stride=heads), :].astype(bf16)
            )


def project_heads(rows_ref, value_ref, count, low, high, first, last, head_dim):
    stacked = jnp.dot(
        rows_ref[first * count : (last + 1) * count, :],
        value_ref[:, low:high],
        preferred_element_type=f32,
    )
    total = jnp.zeros((count, high - low), f32)
    for head in range(first, last + 1):
        part = stacked[(head - first) * count : (head - first + 1) * count, :]
        total = jnp.where(own_head(part.shape, low, head, head_dim), part, total)
    return total


def crop_kernel(
    length_ref,
    token_ref,
    probe_ref,
    owner_ref,
    slot_ref,
    value_hbm,
    send_ref,
    probe_rows,
    maxima_ref,
    total_ref,
    mixed_ref,
    rows_ref,
    value_ref,
    value_sem,
    *,
    capacity,
):
    step = pl.program_id(0)
    block, width, model = token_ref.shape
    heads = probe_ref.shape[1]
    head_dim = model // heads
    crops = owner_ref.shape[1]
    slots = send_ref.shape[0]
    value_copy = pltpu.make_async_copy(value_hbm, value_ref, value_sem)

    @pl.when(step == 0)
    def _():
        value_copy.start()
        probe_rows[...] = probe_ref[...].astype(f32).T.astype(bf16)
        maxima_ref[...] = jnp.zeros(maxima_ref.shape, f32)
        total_ref[...] = jnp.zeros(total_ref.shape, f32)

    tokens = token_ref[...].reshape(block * width, model)
    scores = lax.dot_general(
        probe_rows[...], tokens, contract_last, preferred_element_type=f32
    ) * (1.0 / math.sqrt(head_dim))
    per_group = lanes // width
    lane = iota((heads, lanes), 1)
    maxima = maxima_ref[...]
    totals = total_ref[...]
    weights = []
    for local in range(block):
        group, place = divmod(local, per_group)
        crop = step * block + local
        part = scores[:, group * lanes : (group + 1) * lanes]
        valid = (lane >= place * width) & (lane < place * width + length_ref[0, crop])
        masked = jnp.where(valid, part, very_low)
        peak = jnp.max(masked, axis=1, keepdims=True).astype(bf16).astype(f32)
        weight = jnp.where(valid, jnp.exp(masked - peak), 0.0).astype(bf16)
        amount = jnp.sum(weight.astype(f32), axis=1, keepdims=True)
        maxima = jnp.where(lane == crop, peak, maxima)
        totals = jnp.where(lane == crop, amount, totals)
        weights.append(weight)
    maxima_ref[...] = maxima
    total_ref[...] = totals
    quad = 2 * per_group
    empty = jnp.zeros((heads, lanes), bf16)
    for first in range(0, block, quad):
        rows = [
            jnp.concatenate(
                [weights[first + k], empty] if k < per_group else [empty, weights[first + k]],
                axis=1,
            )
            for k in range(quad)
        ]
        base = pl.multiple_of(step * (block * heads), block * heads) + first * heads
        mixed = jnp.dot(
            jnp.concatenate(rows, axis=0),
            tokens[first * width : (first + quad) * width, :],
            preferred_element_type=f32,
        )
        for part in range(model // lanes):
            mixed_ref[pl.ds(part * crops * heads + base, quad * heads), :] = mixed[
                :, part * lanes : (part + 1) * lanes
            ]

    @pl.when(step == pl.num_programs(0) - 1)
    def _():
        gather_heads(mixed_ref, rows_ref, crops, heads)
        square = (crops, crops)
        owner_row = owner_ref[...]
        owner_column = jnp.sum(
            jnp.where(iota(square, 0) == iota(square, 1), owner_row, 0), axis=1, keepdims=True
        )
        earlier = (owner_column == owner_row) & (iota(square, 0) < iota(square, 1))
        rank = jnp.sum(earlier.astype(jnp.int32), axis=0, keepdims=True)
        place = owner_row * capacity + rank
        member = (iota((slots, crops), 0) == place).astype(bf16)
        total = total_ref[:, :crops]
        coarse = total.astype(bf16).astype(f32)
        row = iota((lanes - 3 * heads, crops), 0)
        extra = jnp.where(
            row == 0, slot_ref[...].astype(f32), jnp.where(row == 1, 1.0, 0.0)
        )
        meta = jnp.concatenate([maxima_ref[:, :crops], coarse, total - coarse, extra], axis=0)
        send_ref[:, model:] = lax.dot_general(
            member, meta.astype(bf16), contract_last, preferred_element_type=f32
        ).astype(bf16)
        value_copy.wait()
        for low, high, first, last in column_tiles(model, head_dim):
            summed = project_heads(rows_ref, value_ref, crops, low, high, first, last, head_dim)
            send_ref[:, low:high] = jnp.dot(
                member, summed.astype(bf16), preferred_element_type=f32
            ).astype(bf16)


def base_kernel(
    token_ref, probe_ref, value_ref, sum_ref, maxima_ref, total_ref, mixed_ref, rows_ref
):
    count, width, model = token_ref.shape
    heads = probe_ref.shape[1]
    head_dim = model // heads
    probe_rows = probe_ref[...].astype(f32).T.astype(bf16)
    per_group = lanes // width
    octet = 2 * per_group
    lane = iota((heads, lanes), 1)
    maxima = jnp.zeros((heads, lanes), f32)
    totals = jnp.zeros((heads, lanes), f32)
    empty = jnp.zeros((heads, lanes), bf16)
    for start in range(0, count, octet):
        tokens = token_ref[start : start + octet].reshape(octet * width, model)
        scores = lax.dot_general(
            probe_rows, tokens, contract_last, preferred_element_type=f32
        ) * (1.0 / math.sqrt(head_dim))
        rows = []
        for local in range(octet):
            group, place = divmod(local, per_group)
            part = scores[:, group * lanes : (group + 1) * lanes]
            valid = (lane >= place * width) & (lane < (place + 1) * width)
            masked = jnp.where(valid, part, very_low)
            peak = jnp.max(masked, axis=1, keepdims=True)
            weight = jnp.where(valid, jnp.exp(masked - peak), 0.0).astype(bf16)
            amount = jnp.sum(weight.astype(f32), axis=1, keepdims=True)
            maxima = jnp.where(lane == start + local, peak, maxima)
            totals = jnp.where(lane == start + local, amount, totals)
            rows.append(
                jnp.concatenate([weight, empty] if group == 0 else [empty, weight], axis=1)
            )
        mixed = jnp.dot(jnp.concatenate(rows, axis=0), tokens, preferred_element_type=f32)
        for part in range(model // lanes):
            base = part * count * heads + start * heads
            mixed_ref[base : base + octet * heads, :] = mixed[:, part * lanes : (part + 1) * lanes]
    maxima_ref[...] = maxima
    total_ref[...] = totals
    gather_heads(mixed_ref, rows_ref, count, heads)
    for low, high, first, last in column_tiles(model, head_dim):
        sum_ref[:, low:high] = project_heads(
            rows_ref, value_ref, count, low, high, first, last, head_dim
        )


def merge_kernel(
    arrived_ref,
    base_ref,
    base_max_ref,
    base_total_ref,
    text_ref,
    label_ref,
    out_weight_hbm,
    embed_ref,
    spread_ref,
    pooled_ref,
    out_weight_ref,
    weight_sem,
):
    count, model = base_ref.shape
    heads = base_max_ref.shape[0]
    head_dim = model // heads
    slots = arrived_ref.shape[0]
    weight_copy = pltpu.make_async_copy(out_weight_hbm, out_weight_ref, weight_sem)
    weight_copy.start()
    square = (lanes, lanes)
    identity = (iota(square, 0) == iota(square, 1)).astype(bf16)
    meta = lax.dot_general(
        identity, arrived_ref[:, model:], contract_last, preferred_element_type=f32
    )
    maxima = meta[:heads]
    totals = meta[heads : 2 * heads] + meta[2 * heads : 3 * heads]
    slot_row = meta[3 * heads : 3 * heads + 1]
    present = meta[3 * heads + 1 : 3 * heads + 2] > 0.5
    base_max = base_max_ref[...]
    lane = iota((heads, lanes), 1)
    joint = jnp.zeros((heads, lanes), f32)
    joint_at = jnp.zeros((heads, slots), f32)
    for image in range(count):
        mine = present & (slot_row == float(image))
        peak = jnp.maximum(
            jnp.max(jnp.where(mine, maxima, very_low), axis=1, keepdims=True),
            base_max[:, image : image + 1],
        )
        joint = jnp.where(lane == image, peak, joint)
        joint_at = jnp.where(mine, peak, joint_at)
    rescale = jnp.where(present, jnp.exp(maxima - joint_at), 0.0).astype(bf16).astype(f32)
    base_rescale = jnp.exp(base_max - joint)
    member = (
        present & (slot_row == iota((count, slots), 0).astype(f32))
    ).astype(f32)
    base_part = jnp.concatenate(
        [base_rescale, base_total_ref[...] * base_rescale, jnp.zeros((lanes - 2 * heads, lanes), f32)],
        axis=0,
    ).T
    base_scale = base_part[:count, :heads]
    denominator = base_part[:count, heads : 2 * heads] + lax.dot_general(
        member, totals * rescale, contract_last, preferred_element_type=f32, precision=highest
    )
    inverse = 1.0 / denominator
    for low, high, first, last in column_tiles(model, head_dim):
        stacked = jnp.dot(
            jnp.concatenate(
                [
                    (member * rescale[head : head + 1, :]).astype(bf16)
                    for head in range(first, last + 1)
                ],
                axis=0,
            ),
            arrived_ref[:, low:high],
            preferred_element_type=f32,
        )
        base_tile = base_ref[:, low:high]
        pooled = jnp.zeros((count, high - low), f32)
        for head in range(first, last + 1):
            part = stacked[(head - first) * count : (head - first + 1) * count, :]
            part = (part + base_tile * base_scale[:, head : head + 1]) * inverse[:, head : head + 1]
            pooled = jnp.where(own_head(part.shape, low, head, head_dim), part, pooled)
        pooled_ref[:, low:high] = pooled.astype(bf16)
    text = text_ref[...].astype(f32)
    text_unit = (
        text * lax.rsqrt(jnp.sum(text * text, axis=1, keepdims=True) + norm_eps)
    ).astype(bf16)
    own = (count, count)
    label_column = jnp.sum(
        jnp.where(iota(own, 0) == iota(own, 1), label_ref[...], 0), axis=1, keepdims=True
    )
    label_lanes = jnp.broadcast_to(label_column.astype(f32), (count, lanes)).astype(bf16)
    weight_copy.wait()
    features = jnp.dot(pooled_ref[...], out_weight_ref[...], preferred_element_type=f32)
    embed_ref[...] = features.astype(bf16)
    image_unit = (
        features * lax.rsqrt(jnp.sum(features * features, axis=1, keepdims=True) + norm_eps)
    ).astype(bf16)
    for peer in range(spread_ref.shape[0]):
        spread_ref[peer, :count, :model] = image_unit
        spread_ref[peer, :count, model:] = jnp.zeros((count, lanes), bf16)
        spread_ref[peer, count:, :model] = text_unit
        spread_ref[peer, count:, model:] = label_lanes


def grad_kernel(
    scale_ref, bias_ref, gathered_ref, own_ref, image_grad_ref, text_grad_ref, image_all, text_all
):
    peers, double, padded = gathered_ref.shape
    count = double // 2
    model = padded - lanes
    labels = []
    for peer in range(peers):
        image_all[peer * count : (peer + 1) * count, :] = gathered_ref[peer, :count, :model]
        text_all[peer * count : (peer + 1) * count, :] = gathered_ref[peer, count:, :model]
        labels.append(gathered_ref[peer, count:, model:])
    first_lane = (iota((8, lanes), 1) == 0).astype(bf16)
    label_row = lax.dot_general(
        first_lane, jnp.concatenate(labels, axis=0), contract_last, preferred_element_type=f32
    )[:1]
    label_column = own_ref[0, count:, model : model + 1].astype(f32)
    scale = scale_ref[0]
    bias = bias_ref[0]
    sign = jnp.where(label_column == label_row, 1.0, -1.0)

    def one_side(own_rows, all_rows, other_rows):
        logits = scale * lax.dot_general(
            own_rows, all_rows[...], contract_last, preferred_element_type=f32
        ) + bias
        tile = (scale * (-sign * jax.nn.sigmoid(-sign * logits))).astype(bf16)
        return jnp.dot(tile, other_rows[...], preferred_element_type=f32)

    image_grad_ref[...] = one_side(own_ref[0, :count, :model], text_all, text_all)
    text_grad_ref[...] = one_side(own_ref[0, count:, :model], image_all, image_all)


def per_device(
    crop_tokens,
    crop_lengths,
    crop_owner,
    crop_slot,
    base_tokens,
    key_probe,
    value_weight,
    out_weight,
    text_embed,
    pair_labels,
    logit_scale,
    logit_bias,
):
    owners = lax.axis_size("dp")
    peers = lax.axis_size("loop")
    crops, width, model = crop_tokens.shape
    count = base_tokens.shape[0]
    heads = key_probe.shape[1]
    capacity = max(2, (2 * crops + owners - 1) // owners)
    slots = owners * capacity
    padded = model + lanes
    block = 8
    vmem = pl.BlockSpec(memory_space=pltpu.VMEM)
    smem = pl.BlockSpec(memory_space=pltpu.SMEM)
    anywhere = pl.BlockSpec(memory_space=pl.ANY)
    whole = lambda *shape: pl.BlockSpec(shape, lambda step, lengths: (0,) * len(shape))

    def crop_body(*refs):
        crop_kernel(*refs, capacity=capacity)

    send = pl.pallas_call(
        crop_body,
        grid_spec=pltpu.PrefetchScalarGridSpec(
            num_scalar_prefetch=1,
            grid=(crops // block,),
            in_specs=[
                pl.BlockSpec((block, width, model), lambda step, lengths: (step, 0, 0)),
                whole(model, heads),
                whole(1, crops),
                whole(1, crops),
                anywhere,
            ],
            out_specs=whole(slots, padded),
            scratch_shapes=[
                pltpu.VMEM((heads, model), bf16),
                pltpu.VMEM((heads, lanes), f32),
                pltpu.VMEM((heads, lanes), f32),
                pltpu.VMEM((model // lanes * crops * heads, lanes), f32),
                pltpu.VMEM((crops * heads, model), bf16),
                pltpu.VMEM((model, model), bf16),
                pltpu.SemaphoreType.DMA,
            ],
        ),
        out_shape=jax.ShapeDtypeStruct((slots, padded), bf16),
        name="crop_partial",
    )(
        crop_lengths,
        crop_tokens,
        key_probe,
        crop_owner.reshape(1, crops),
        crop_slot.reshape(1, crops),
        value_weight,
    )
    arrived = lax.all_to_all(send, "dp", split_axis=0, concat_axis=0, tiled=True)
    base_sum, base_max, base_total = pl.pallas_call(
        base_kernel,
        in_specs=[vmem] * 3,
        out_specs=[vmem] * 3,
        out_shape=[
            jax.ShapeDtypeStruct((count, model), f32),
            jax.ShapeDtypeStruct((heads, lanes), f32),
            jax.ShapeDtypeStruct((heads, lanes), f32),
        ],
        scratch_shapes=[
            pltpu.VMEM((model // lanes * count * heads, lanes), f32),
            pltpu.VMEM((count * heads, model), bf16),
        ],
        name="base_partial",
    )(base_tokens, key_probe, value_weight)
    image_embed, spread = pl.pallas_call(
        merge_kernel,
        in_specs=[vmem] * 6 + [anywhere],
        out_specs=[vmem] * 2,
        out_shape=[
            jax.ShapeDtypeStruct((count, model), bf16),
            jax.ShapeDtypeStruct((peers, 2 * count, padded), bf16),
        ],
        scratch_shapes=[
            pltpu.VMEM((count, model), bf16),
            pltpu.VMEM((model, model), bf16),
            pltpu.SemaphoreType.DMA,
        ],
        name="merge_parts",
    )(
        arrived,
        base_sum,
        base_max,
        base_total,
        text_embed,
        pair_labels.reshape(1, count),
        out_weight,
    )
    gathered = lax.all_to_all(spread, "loop", split_axis=0, concat_axis=0, tiled=True)
    image_grad, text_grad = pl.pallas_call(
        grad_kernel,
        in_specs=[smem, smem, vmem, vmem],
        out_specs=[vmem] * 2,
        out_shape=[
            jax.ShapeDtypeStruct((count, model), f32),
            jax.ShapeDtypeStruct((count, model), f32),
        ],
        scratch_shapes=[
            pltpu.VMEM((peers * count, model), bf16),
            pltpu.VMEM((peers * count, model), bf16),
        ],
        name="loss_grads",
    )(logit_scale, logit_bias, gathered, spread)
    return (image_embed, image_grad, text_grad)


def solution(mesh):
    return jax.shard_map(
        per_device,
        mesh=mesh,
        in_specs=(
            P(("dp", "loop"), None, None),
            P(("dp", "loop"), None),
            P(("dp", "loop"), None),
            P(("dp", "loop")),
            P(("dp", "loop"), None, None),
            P(),
            P(),
            P(),
            P(("dp", "loop"), None),
            P(("dp", "loop")),
            P(),
            P(),
        ),
        out_specs=(P(("dp", "loop"), None), P(("dp", "loop"), None), P(("dp", "loop"), None)),
        check_vma=False,
    )
```

```python
import math

import jax
import jax.numpy as jnp
from jax import lax
from jax.experimental import pallas as pl
from jax.experimental.pallas import tpu as pltpu
from jax.sharding import PartitionSpec as P

very_low = -1e30
norm_eps = 1e-06
highest = lax.Precision.HIGHEST
f32 = jnp.float32
bf16 = jnp.bfloat16
contract_last = (((1,), (1,)), ((), ()))
lanes = 128
sublanes = 8
col_tile = 256
token_tile = 256


def iota(shape, dim):
    return lax.broadcasted_iota(jnp.int32, shape, dim)


def head_lane(lane, heads, per_tile):
    return (lane % (heads // per_tile)) * per_tile + lane // (heads // per_tile)


def score_rows(probe_rows, tokens, head_dim):
    return lax.dot_general(
        probe_rows, tokens, contract_last, preferred_element_type=f32
    ) * (1.0 / math.sqrt(head_dim))


def weighted_rows(scores, tokens, valid, rows_ref, block, stride, units, rounded):
    heads = scores.shape[0]
    per_tile = sublanes // units
    tiles = heads // per_tile
    row = iota(valid.shape, 0)
    lane = iota((sublanes, lanes), 1)
    peaks = jnp.zeros((sublanes, lanes), f32)
    totals = jnp.zeros((sublanes, lanes), f32)
    weights = []
    for tile in range(tiles):
        part = jnp.broadcast_to(scores[tile * per_tile : tile * per_tile + 1, :], valid.shape)
        for k in range(1, per_tile):
            head = tile * per_tile + k
            part = jnp.where(row >= k * units, scores[head : head + 1, :], part)
        masked = jnp.where(valid, part, very_low)
        peak = jnp.max(masked, axis=1, keepdims=True)
        if rounded:
            peak = peak.astype(bf16).astype(f32)
        weight = jnp.exp(masked - peak).astype(bf16).astype(f32)
        amount = jnp.sum(weight, axis=1, keepdims=True)
        peaks = jnp.where(lane == tile, peak, peaks)
        totals = jnp.where(lane == tile, amount, totals)
        weights.append(weight)
    mixed = jnp.dot(
        jnp.concatenate(weights, axis=0).astype(bf16), tokens, preferred_element_type=f32
    )
    for tile in range(tiles):
        start = tile * stride + block * sublanes
        if not isinstance(start, int):
            start = pl.multiple_of(start, sublanes)
        rows_ref[pl.ds(start, sublanes), :] = mixed[tile * sublanes : (tile + 1) * sublanes, :]
    row = iota((sublanes, lanes), 0)
    for k in range(1, per_tile):
        peaks = jnp.where(row >= k * units, jnp.roll(peaks, k * tiles, axis=1), peaks)
        totals = jnp.where(row >= k * units, jnp.roll(totals, k * tiles, axis=1), totals)
    return peaks, totals


def project_heads(rows_ref, value_ref, stride, low, high, head_dim, units):
    per_tile = sublanes // units
    first = low // head_dim // per_tile
    last = (high - 1) // head_dim // per_tile
    stacked = jnp.dot(
        rows_ref[first * stride : (last + 1) * stride, :].astype(bf16),
        value_ref[:, low:high],
        preferred_element_type=f32,
    )
    shape = (stride, high - low)
    kind = iota(shape, 0) % sublanes // units
    column = iota(shape, 1) + low - kind * head_dim
    total = jnp.zeros(shape, f32)
    for tile in range(first, last + 1):
        start = tile * per_tile * head_dim
        mine = (column >= start) & (column < start + head_dim)
        total = jnp.where(
            mine, stacked[(tile - first) * stride : (tile - first + 1) * stride, :], total
        )
    return total


def column_of(row):
    square = (row.shape[1], row.shape[1])
    return jnp.sum(jnp.where(iota(square, 0) == iota(square, 1), row, 0), axis=1, keepdims=True)


def crop_kernel(
    token_hbm,
    probe_ref,
    length_ref,
    owner_ref,
    slot_ref,
    value_hbm,
    send_ref,
    token_ref,
    rows_ref,
    meta_ref,
    limit_ref,
    value_ref,
    token_sem,
    value_sem,
    *,
    capacity,
):
    crops, width, model = token_ref.shape
    heads = probe_ref.shape[0]
    head_dim = model // heads
    slots = send_ref.shape[0]
    units = token_tile // width
    per_tile = sublanes // units
    rows = crops * per_tile
    blocks = token_sem.shape[0]
    per_step = crops // blocks
    parts = per_step // units

    def token_copy(step):
        where = pl.ds(step * per_step, per_step)
        return pltpu.make_async_copy(token_hbm.at[where], token_ref.at[where], token_sem.at[step])

    for step in range(blocks):
        token_copy(step).start()
    value_copy = pltpu.make_async_copy(value_hbm, value_ref, value_sem)
    value_copy.start()
    expand = (rows, crops)
    owner_of = iota(expand, 0) // sublanes * units + iota(expand, 0) % units
    chosen = owner_of == iota(expand, 1)
    limit_ref[...] = jnp.broadcast_to(
        jnp.sum(jnp.where(chosen, length_ref[...], 0), axis=1, keepdims=True), limit_ref.shape
    )
    wide = (sublanes, token_tile)
    offset = iota(wide, 1) - iota(wide, 0) % units * width

    def tokens_of(step, part):
        start = step * per_step + part * units
        return token_ref[pl.ds(start, units)].reshape(units * width, model)

    def scores_of(step):
        return tuple(
            score_rows(probe_ref[...], tokens_of(step, part), head_dim) for part in range(parts)
        )

    def pool(step, scores):
        for part in range(parts):
            block = step * parts + part
            start = pl.multiple_of(block * sublanes, sublanes)
            limit = jnp.concatenate(
                [limit_ref[pl.ds(start, sublanes), :]] * (token_tile // lanes), axis=1
            )
            peaks, totals = weighted_rows(
                scores[part],
                tokens_of(step, part),
                (offset >= 0) & (offset < limit),
                rows_ref,
                block,
                rows,
                units,
                True,
            )
            coarse = totals.astype(bf16).astype(f32)
            meta_ref[pl.ds(start, sublanes), :] = (
                peaks
                + jnp.roll(coarse, heads, axis=1)
                + jnp.roll(totals - coarse, 2 * heads, axis=1)
            )

    token_copy(0).wait()

    def advance(step, scores):
        token_copy(step + 1).wait()
        following = scores_of(step + 1)
        pool(step, scores)
        return following

    pool(blocks - 1, lax.fori_loop(0, blocks - 1, advance, scores_of(0)))

    owner_row = owner_ref[...]
    square = (crops, crops)
    earlier = (column_of(owner_row) == owner_row) & (iota(square, 0) < iota(square, 1))
    rank = jnp.sum(earlier.astype(jnp.int32), axis=0, keepdims=True)
    place = owner_row * capacity + rank
    place_row = jnp.sum(
        jnp.where(
            iota((crops, rows), 1) // sublanes * units + iota((crops, rows), 1) % units
            == iota((crops, rows), 0),
            column_of(place),
            0,
        ),
        axis=0,
        keepdims=True,
    )
    member = (iota((slots, rows), 0) == place_row).astype(bf16)
    slot_of = jnp.sum(jnp.where(chosen, slot_ref[...], 0), axis=1, keepdims=True)
    lane = iota((rows, lanes), 1)
    lead = iota((rows, lanes), 0) % sublanes < units
    extra = jnp.where(lane == 3 * heads, slot_of.astype(f32), 0.0) + jnp.where(
        lane == 3 * heads + 1, 1.0, 0.0
    )
    meta = meta_ref[...] + jnp.where(lead, extra, 0.0)
    send_ref[:, model:] = jnp.dot(
        member, meta.astype(bf16), preferred_element_type=f32
    ).astype(bf16)
    value_copy.wait()
    for low in range(0, model, col_tile):
        high = min(low + col_tile, model)
        summed = project_heads(rows_ref, value_ref, rows, low, high, head_dim, units)
        send_ref[:, low:high] = jnp.dot(
            member, summed.astype(bf16), preferred_element_type=f32
        ).astype(bf16)


def base_kernel(
    token_hbm,
    probe_ref,
    value_hbm,
    sum_ref,
    peak_ref,
    total_ref,
    token_ref,
    rows_ref,
    value_ref,
    token_sem,
    value_sem,
    *,
    per_tile,
):
    count, width, model = token_ref.shape
    heads = probe_ref.shape[0]
    head_dim = model // heads
    units = token_tile // width
    blocks = count // units
    copies = []
    for block in range(blocks):
        where = pl.ds(block * units, units)
        copies.append(
            pltpu.make_async_copy(token_hbm.at[where], token_ref.at[where], token_sem.at[block])
        )
        copies[-1].start()
    value_copy = pltpu.make_async_copy(value_hbm, value_ref, value_sem)
    value_copy.start()
    wide = (sublanes, token_tile)
    offset = iota(wide, 1) - iota(wide, 0) * width
    valid = (offset >= 0) & (offset < width)
    lane = iota((lanes, lanes), 1)
    order = (head_lane(lane, heads, per_tile) == iota((lanes, lanes), 0)) & (lane < heads)
    stats = []
    for block in range(blocks):
        copies[block].wait()
        tokens = token_ref[block * units : (block + 1) * units].reshape(units * width, model)
        scores = score_rows(probe_ref[...], tokens, head_dim)
        stats.append(
            weighted_rows(scores, tokens, valid, rows_ref, block, count, units, False)
        )
    for index, out_ref in ((0, peak_ref), (1, total_ref)):
        out_ref[...] = jnp.dot(
            jnp.concatenate([pair[index] for pair in stats], axis=0),
            order.astype(f32),
            preferred_element_type=f32,
            precision=highest,
        )
    value_copy.wait()
    for low in range(0, model, col_tile):
        high = min(low + col_tile, model)
        sum_ref[:, low:high] = project_heads(
            rows_ref, value_ref, count, low, high, head_dim, units
        )


def two_part_dot(matrix, table):
    coarse = matrix.astype(bf16)
    fine = (matrix - coarse.astype(f32)).astype(bf16)
    return jnp.dot(coarse, table, preferred_element_type=f32) + jnp.dot(
        fine, table, preferred_element_type=f32
    )


def merge_kernel(
    arrived_ref,
    base_ref,
    base_peak_ref,
    base_total_ref,
    text_ref,
    label_ref,
    out_weight_ref,
    embed_ref,
    own_ref,
    peak_ref,
    *,
    heads,
    per_tile,
):
    count, model = base_ref.shape
    head_dim = model // heads
    slots = arrived_ref.shape[0]
    meta = arrived_ref[:, model:].astype(f32)
    slot_column = jnp.where(
        meta[:, 3 * heads + 1 : 3 * heads + 2] > 0.5, meta[:, 3 * heads : 3 * heads + 1], -1.0
    )
    slot_wide = jnp.broadcast_to(slot_column, (slots, lanes))
    for image in range(count):
        peak_ref[image : image + 1, :] = jnp.max(
            jnp.where(slot_wide == float(image), meta, very_low), axis=0, keepdims=True
        )
    base_peak = base_peak_ref[...]
    joint = jnp.maximum(peak_ref[...], base_peak)
    member = (slot_column == iota((slots, count), 1).astype(f32)).astype(f32)
    joint_at = jnp.dot(member, joint, preferred_element_type=f32, precision=highest)
    used = (iota((slots, lanes), 1) < heads) & (slot_wide >= 0.0)
    rescale = jnp.where(used, jnp.exp(jnp.where(used, meta - joint_at, 0.0)), 0.0).astype(bf16)
    totals = jnp.roll(meta, -heads, axis=1) + jnp.roll(meta, -2 * heads, axis=1)
    lane = iota((count, lanes), 1)
    base_rescale = jnp.where(lane < heads, jnp.exp(base_peak - joint), 0.0)
    collected = lax.dot_general(
        member,
        totals * rescale.astype(f32),
        (((0,), (0,)), ((), ())),
        preferred_element_type=f32,
        precision=highest,
    )
    inverse = 1.0 / (collected + base_total_ref[...] * base_rescale + jnp.where(lane < heads, 0.0, 1.0))
    table_shape = (lanes, model)
    table_row = iota(table_shape, 0)
    column = iota(table_shape, 1) - head_lane(table_row, heads, per_tile) * head_dim
    table = ((column >= 0) & (column < head_dim) & (table_row < heads)).astype(bf16)
    scaled = arrived_ref[:, :model].astype(f32) * jnp.dot(
        rescale, table, preferred_element_type=f32
    )
    crop_sum = lax.dot_general(
        member.astype(bf16),
        scaled.astype(bf16),
        (((0,), (0,)), ((), ())),
        preferred_element_type=f32,
    )
    factors = two_part_dot(jnp.concatenate([inverse, base_rescale * inverse], axis=0), table)
    pooled = (crop_sum * factors[:count] + base_ref[...] * factors[count:]).astype(bf16)
    text = text_ref[...].astype(f32)
    text_unit = (
        text * lax.rsqrt(jnp.sum(text * text, axis=1, keepdims=True) + norm_eps)
    ).astype(bf16)
    double = 2 * count
    for part in range(model // lanes):
        own_ref[part * double + count : (part + 1) * double, :] = text_unit[
            :, part * lanes : (part + 1) * lanes
        ]
    own_ref[model // lanes * double :, :] = jnp.broadcast_to(
        jnp.concatenate([label_ref[...].astype(f32)] * (lanes // count), axis=1),
        (own_ref.shape[0] - model // lanes * double, lanes),
    ).astype(bf16)
    features = jnp.dot(pooled, out_weight_ref[...], preferred_element_type=f32)
    embed_ref[...] = features.astype(bf16)
    image_unit = (
        features * lax.rsqrt(jnp.sum(features * features, axis=1, keepdims=True) + norm_eps)
    ).astype(bf16)
    for part in range(model // lanes):
        own_ref[part * double : part * double + count, :] = image_unit[
            :, part * lanes : (part + 1) * lanes
        ]


def grad_kernel(scale_ref, bias_ref, label_ref, *refs):
    pieces, (image_grad_ref, text_grad_ref, everyone) = refs[:-3], refs[-3:]
    count, model = image_grad_ref.shape
    double = 2 * count
    parts = model // lanes
    label_rows = []
    for index, piece in enumerate(pieces):
        for part in range(parts):
            everyone[
                index * double : (index + 1) * double, part * lanes : (part + 1) * lanes
            ] = piece[part * double : (part + 1) * double, :]
        label_rows.append(piece[parts * double :, :].astype(f32)[:1])
    lane = iota((1, lanes), 1)
    per_row = lanes // double
    label_row = []
    for first in range(0, len(pieces), per_row):
        row = label_rows[first]
        for k in range(1, per_row):
            row = jnp.where(lane >= k * double, label_rows[first + k], row)
        label_row.append(row)
    label_row = jnp.concatenate(label_row, axis=1)
    label_column = column_of(label_ref[...]).astype(f32)
    label_column = jnp.concatenate([label_column, label_column], axis=0)
    scale = scale_ref[0]
    bias = bias_ref[0]
    sign = jnp.where(label_column == label_row, 1.0, -1.0)
    logits = scale * lax.dot_general(
        everyone[:double, :], everyone[...], contract_last, preferred_element_type=f32
    ) + bias
    tile = scale * (-sign * jax.nn.sigmoid(-sign * logits))
    other_side = (iota(tile.shape, 1) % double >= count) == (iota(tile.shape, 0) < count)
    tile = jnp.where(other_side, tile, 0.0).astype(bf16)
    grads = jnp.dot(tile, everyone[...], preferred_element_type=f32)
    image_grad_ref[...] = grads[:count]
    text_grad_ref[...] = grads[count:]


def per_device(
    crop_tokens,
    crop_lengths,
    crop_owner,
    crop_slot,
    base_tokens,
    key_probe,
    value_weight,
    out_weight,
    text_embed,
    pair_labels,
    logit_scale,
    logit_bias,
):
    owners = lax.axis_size("dp")
    peers = lax.axis_size("loop")
    crops, width, model = crop_tokens.shape
    count, base_width, _ = base_tokens.shape
    heads = key_probe.shape[1]
    capacity = max(2, (2 * crops + owners - 1) // owners)
    slots = owners * capacity
    padded = model + lanes
    blocks = 8
    per_tile = sublanes * width // token_tile
    rows = crops * per_tile
    payload = (model // lanes * 2 * count + 16, lanes)
    vmem = pl.BlockSpec(memory_space=pltpu.VMEM)
    smem = pl.BlockSpec(memory_space=pltpu.SMEM)
    anywhere = pl.BlockSpec(memory_space=pl.ANY)
    probe_rows = key_probe.T

    def crop_body(*refs):
        crop_kernel(*refs, capacity=capacity)

    def base_body(*refs):
        base_kernel(*refs, per_tile=per_tile)

    def merge_body(*refs):
        merge_kernel(*refs, heads=heads, per_tile=per_tile)

    send = pl.pallas_call(
        crop_body,
        in_specs=[anywhere, vmem, vmem, vmem, vmem, anywhere],
        out_specs=vmem,
        scratch_shapes=[
            pltpu.VMEM((crops, width, model), bf16),
            pltpu.VMEM((crops * heads, model), f32),
            pltpu.VMEM((rows, lanes), f32),
            pltpu.VMEM((rows, lanes), jnp.int32),
            pltpu.VMEM((model, model), bf16),
            pltpu.SemaphoreType.DMA((blocks,)),
            pltpu.SemaphoreType.DMA,
        ],
        out_shape=jax.ShapeDtypeStruct((slots, padded), bf16),
        name="crop_partial",
    )(
        crop_tokens,
        probe_rows,
        crop_lengths,
        crop_owner.reshape(1, crops),
        crop_slot.reshape(1, crops),
        value_weight,
    )
    arrived = lax.all_to_all(send, "dp", split_axis=0, concat_axis=0, tiled=True)
    arrived = pltpu.with_memory_space_constraint(arrived, pltpu.VMEM)
    base_sum, base_peak, base_total = pl.pallas_call(
        base_body,
        in_specs=[anywhere, vmem, anywhere],
        out_specs=[vmem] * 3,
        out_shape=[
            jax.ShapeDtypeStruct((count, model), f32),
            jax.ShapeDtypeStruct((count, lanes), f32),
            jax.ShapeDtypeStruct((count, lanes), f32),
        ],
        scratch_shapes=[
            pltpu.VMEM((count, base_width, model), bf16),
            pltpu.VMEM((count * heads, model), f32),
            pltpu.VMEM((model, model), bf16),
            pltpu.SemaphoreType.DMA((count * base_width // token_tile,)),
            pltpu.SemaphoreType.DMA,
        ],
        name="base_partial",
    )(base_tokens, probe_rows, value_weight)
    label_row = pair_labels.reshape(1, count)
    image_embed, own = pl.pallas_call(
        merge_body,
        in_specs=[vmem] * 7,
        out_specs=[vmem] * 2,
        out_shape=[
            jax.ShapeDtypeStruct((count, model), bf16),
            jax.ShapeDtypeStruct(payload, bf16),
        ],
        scratch_shapes=[pltpu.VMEM((count, lanes), f32)],
        name="merge_parts",
    )(
        arrived,
        base_sum,
        base_peak,
        base_total,
        text_embed,
        label_row,
        pltpu.with_memory_space_constraint(out_weight, pltpu.VMEM),
    )

    def peer_copy(array, half, turn):
        column = peers // 2
        pairs = [
            (p, (p // column ^ half) * column + (p % column + turn) % column) for p in range(peers)
        ]
        return lax.ppermute(array, "loop", pairs)

    other = peer_copy(own, 1, 0)
    turns = (1, 3, 2)
    pieces = [own, other]
    pieces += [peer_copy(own, 0, turn) for turn in turns]
    pieces += [peer_copy(other, 0, turn) for turn in turns]
    pieces = [pltpu.with_memory_space_constraint(piece, pltpu.VMEM) for piece in pieces]
    image_grad, text_grad = pl.pallas_call(
        grad_kernel,
        in_specs=[smem, smem, vmem] + [vmem] * peers,
        out_specs=[vmem] * 2,
        out_shape=[
            jax.ShapeDtypeStruct((count, model), f32),
            jax.ShapeDtypeStruct((count, model), f32),
        ],
        scratch_shapes=[pltpu.VMEM((peers * 2 * count, model), bf16)],
        name="loss_grads",
    )(logit_scale, logit_bias, label_row, *pieces)
    return (image_embed, image_grad, text_grad)


def solution(mesh):
    return jax.shard_map(
        per_device,
        mesh=mesh,
        in_specs=(
            P(("dp", "loop"), None, None),
            P(("dp", "loop"), None),
            P(("dp", "loop"), None),
            P(("dp", "loop")),
            P(("dp", "loop"), None, None),
            P(),
            P(),
            P(),
            P(("dp", "loop"), None),
            P(("dp", "loop")),
            P(),
            P(),
        ),
        out_specs=(P(("dp", "loop"), None), P(("dp", "loop"), None), P(("dp", "loop"), None)),
        check_vma=False,
    )
```

```python
import math

import jax
import jax.numpy as jnp
from jax import lax
from jax.experimental import pallas as pl
from jax.experimental.pallas import tpu as pltpu
from jax.sharding import PartitionSpec as P

very_low = -1e30
norm_eps = 1e-06
highest = lax.Precision.HIGHEST
f32 = jnp.float32
bf16 = jnp.bfloat16
contract_last = (((1,), (1,)), ((), ()))
lanes = 128
sublanes = 8
col_tile = 256
token_tile = 256


def iota(shape, dim):
    return lax.broadcasted_iota(jnp.int32, shape, dim)


def head_lane(lane, heads, per_tile):
    return (lane % (heads // per_tile)) * per_tile + lane // (heads // per_tile)


def score_rows(probe_rows, tokens, head_dim):
    return lax.dot_general(
        probe_rows, tokens, contract_last, preferred_element_type=f32
    ) * (1.0 / math.sqrt(head_dim))


def softmax_rows(scores, valid, units, rounded):
    heads = scores.shape[0]
    per_tile = sublanes // units
    tiles = heads // per_tile
    row = iota(valid.shape, 0)
    lane = iota((sublanes, lanes), 1)
    peaks = jnp.zeros((sublanes, lanes), f32)
    totals = jnp.zeros((sublanes, lanes), f32)
    weights = []
    for tile in range(tiles):
        part = jnp.broadcast_to(scores[tile * per_tile : tile * per_tile + 1, :], valid.shape)
        for k in range(1, per_tile):
            head = tile * per_tile + k
            part = jnp.where(row >= k * units, scores[head : head + 1, :], part)
        masked = jnp.where(valid, part, very_low)
        peak = jnp.max(masked, axis=1, keepdims=True)
        if rounded:
            peak = peak.astype(bf16).astype(f32)
        weight = jnp.exp(masked - peak).astype(bf16).astype(f32)
        amount = jnp.sum(weight, axis=1, keepdims=True)
        peaks = jnp.where(lane == tile, peak, peaks)
        totals = jnp.where(lane == tile, amount, totals)
        weights.append(weight)
    row = iota((sublanes, lanes), 0)
    for k in range(1, per_tile):
        peaks = jnp.where(row >= k * units, jnp.roll(peaks, k * tiles, axis=1), peaks)
        totals = jnp.where(row >= k * units, jnp.roll(totals, k * tiles, axis=1), totals)
    return jnp.concatenate(weights, axis=0).astype(bf16), peaks, totals


def mix_rows(rows_ref, stride, step, weights, tokens):
    mixed = [
        jnp.dot(weight, token, preferred_element_type=f32)
        for weight, token in zip(weights, tokens)
    ]
    height = len(mixed) * sublanes
    for tile in range(mixed[0].shape[0] // sublanes):
        start = tile * stride + step * height
        if not isinstance(start, int):
            start = pl.multiple_of(start, height)
        rows_ref[pl.ds(start, height), :] = jnp.concatenate(
            [part[tile * sublanes : (tile + 1) * sublanes, :] for part in mixed], axis=0
        ).astype(bf16)


def project_tile(rows_ref, value_ref, stride, low, high, head_dim, units):
    span = sublanes // units * head_dim
    first = low // span
    last = (high - 1) // span
    stacked = jnp.dot(
        rows_ref[first * stride : (last + 1) * stride, :],
        value_ref[:, low:high],
        preferred_element_type=f32,
    ).reshape(last + 1 - first, stride // sublanes, sublanes, high - low)
    shape = (1, sublanes, high - low)
    kind = iota(shape, 1) // units
    column = iota(shape, 2) + low - kind * head_dim
    total = jnp.where(column >= first * span, stacked[0], 0.0)
    for tile in range(first + 1, last + 1):
        total = jnp.where(column >= tile * span, stacked[tile - first], total)
    if units < sublanes:
        owner = (column >= 0) & (column % span < head_dim)
        total = jnp.where(owner, total, 0.0)
    return total.reshape(stride, high - low)


def project_heads(rows_ref, value_ref, stride, model, head_dim, units, finish):
    waiting = None
    for low in range(0, model, col_tile):
        high = min(low + col_tile, model)
        current = project_tile(rows_ref, value_ref, stride, low, high, head_dim, units)
        if waiting is not None:
            finish(*waiting)
        waiting = (low, high, current)
    finish(*waiting)


def column_of(row):
    square = (row.shape[1], row.shape[1])
    return jnp.sum(jnp.where(iota(square, 0) == iota(square, 1), row, 0), axis=1, keepdims=True)


def crop_kernel(
    token_hbm,
    probe_ref,
    length_ref,
    owner_ref,
    slot_ref,
    value_hbm,
    send_ref,
    token_ref,
    rows_ref,
    meta_ref,
    limit_ref,
    member_ref,
    value_ref,
    token_sem,
    value_sem,
    *,
    capacity,
):
    crops, width, model = token_ref.shape
    heads = probe_ref.shape[0]
    head_dim = model // heads
    slots = send_ref.shape[0]
    units = token_tile // width
    per_tile = sublanes // units
    rows = crops * per_tile
    blocks = token_sem.shape[0]
    per_step = crops // blocks
    parts = per_step // units

    def token_copy(step):
        where = pl.ds(step * per_step, per_step)
        return pltpu.make_async_copy(token_hbm.at[where], token_ref.at[where], token_sem.at[step])

    for step in range(blocks):
        token_copy(step).start()
    value_copy = pltpu.make_async_copy(value_hbm, value_ref, value_sem)
    value_copy.start()
    expand = (rows, crops)
    owner_of = iota(expand, 0) // sublanes * units + iota(expand, 0) % units
    chosen = owner_of == iota(expand, 1)
    limit_ref[...] = jnp.broadcast_to(
        jnp.sum(jnp.where(chosen, length_ref[...], 0), axis=1, keepdims=True), limit_ref.shape
    )
    wide = (sublanes, token_tile)
    offset = iota(wide, 1) - iota(wide, 0) % units * width

    def tokens_of(step, part):
        start = step * per_step + part * units
        return token_ref[pl.ds(start, units)].reshape(units * width, model)

    owner_row = owner_ref[...]
    square = (crops, crops)
    earlier = (column_of(owner_row) == owner_row) & (iota(square, 0) < iota(square, 1))
    rank = jnp.sum(earlier.astype(jnp.int32), axis=0, keepdims=True)
    place = owner_row * capacity + rank
    turned = (crops, rows)
    place_row = jnp.sum(
        jnp.where(
            iota(turned, 1) // sublanes * units + iota(turned, 1) % units == iota(turned, 0),
            column_of(place),
            0,
        ),
        axis=0,
        keepdims=True,
    )
    member_ref[...] = (iota((slots, rows), 0) == place_row).astype(bf16)
    slot_of = jnp.sum(jnp.where(chosen, slot_ref[...], 0), axis=1, keepdims=True)
    lane = iota((rows, lanes), 1)
    lead = iota((rows, lanes), 0) % sublanes < units
    extra = jnp.where(lane == 3 * heads, slot_of.astype(f32), 0.0) + jnp.where(
        lane == 3 * heads + 1, 1.0, 0.0
    )
    meta_ref[...] = jnp.where(lead, extra, 0.0)

    def scores_of(step):
        return tuple(
            score_rows(probe_ref[...], tokens_of(step, part), head_dim) for part in range(parts)
        )

    def weigh(step, scores):
        weights = []
        for part in range(parts):
            start = pl.multiple_of((step * parts + part) * sublanes, sublanes)
            limit = jnp.concatenate(
                [limit_ref[pl.ds(start, sublanes), :]] * (token_tile // lanes), axis=1
            )
            weight, peaks, totals = softmax_rows(
                scores[part], (offset >= 0) & (offset < limit), units, True
            )
            coarse = totals.astype(bf16).astype(f32)
            meta_ref[pl.ds(start, sublanes), :] += (
                peaks
                + jnp.roll(coarse, heads, axis=1)
                + jnp.roll(totals - coarse, 2 * heads, axis=1)
            )
            weights.append(weight)
        return tuple(weights)

    def mix(step, weights):
        mix_rows(
            rows_ref, rows, step, weights, [tokens_of(step, part) for part in range(parts)]
        )

    token_copy(0).wait()
    scores = scores_of(0)
    token_copy(1).wait()
    following = scores_of(1)
    weights = weigh(0, scores)

    def advance(step, carry):
        scores, weights = carry
        token_copy(step + 1).wait()
        mix(step - 1, weights)
        following = scores_of(step + 1)
        return following, weigh(step, scores)

    scores, weights = lax.fori_loop(1, blocks - 1, advance, (following, weights))
    mix(blocks - 2, weights)
    mix(blocks - 1, weigh(blocks - 1, scores))
    send_ref[:, model:] = jnp.dot(
        member_ref[...], meta_ref[...].astype(bf16), preferred_element_type=f32
    ).astype(bf16)
    value_copy.wait()

    def finish(low, high, summed):
        send_ref[:, low:high] = jnp.dot(
            member_ref[...], summed.astype(bf16), preferred_element_type=f32
        ).astype(bf16)

    project_heads(rows_ref, value_ref, rows, model, head_dim, units, finish)


def base_kernel(
    token_hbm,
    probe_ref,
    value_hbm,
    sum_ref,
    peak_ref,
    total_ref,
    token_ref,
    rows_ref,
    value_ref,
    token_sem,
    value_sem,
    *,
    per_tile,
):
    count, width, model = token_ref.shape
    heads = probe_ref.shape[0]
    head_dim = model // heads
    units = token_tile // width
    blocks = count // units
    copies = []
    for block in range(blocks):
        where = pl.ds(block * units, units)
        copies.append(
            pltpu.make_async_copy(token_hbm.at[where], token_ref.at[where], token_sem.at[block])
        )
        copies[-1].start()
    value_copy = pltpu.make_async_copy(value_hbm, value_ref, value_sem)
    value_copy.start()
    wide = (sublanes, token_tile)
    offset = iota(wide, 1) - iota(wide, 0) * width
    valid = (offset >= 0) & (offset < width)
    lane = iota((lanes, lanes), 1)
    order = (head_lane(lane, heads, per_tile) == iota((lanes, lanes), 0)) & (lane < heads)
    stats = []
    weights = []
    tokens = []
    for block in range(blocks):
        copies[block].wait()
        tokens.append(
            token_ref[block * units : (block + 1) * units].reshape(units * width, model)
        )
        scores = score_rows(probe_ref[...], tokens[block], head_dim)
        weight, peaks, totals = softmax_rows(scores, valid, units, False)
        weights.append(weight)
        stats.append((peaks, totals))
        if block % 2 == 1:
            pair = slice(block - 1, block + 1)
            mix_rows(rows_ref, count, block // 2, weights[pair], tokens[pair])
    for index, out_ref in ((0, peak_ref), (1, total_ref)):
        out_ref[...] = jnp.dot(
            jnp.concatenate([pair[index] for pair in stats], axis=0),
            order.astype(f32),
            preferred_element_type=f32,
            precision=highest,
        )
    value_copy.wait()

    def finish(low, high, summed):
        sum_ref[:, low:high] = summed

    project_heads(rows_ref, value_ref, count, model, head_dim, units, finish)


def two_part_dot(matrix, table):
    coarse = matrix.astype(bf16)
    fine = (matrix - coarse.astype(f32)).astype(bf16)
    return jnp.dot(coarse, table, preferred_element_type=f32) + jnp.dot(
        fine, table, preferred_element_type=f32
    )


def merge_kernel(
    arrived_ref,
    base_ref,
    base_peak_ref,
    base_total_ref,
    text_ref,
    label_ref,
    out_weight_ref,
    embed_ref,
    own_ref,
    peak_ref,
    *,
    heads,
    per_tile,
):
    count, model = base_ref.shape
    head_dim = model // heads
    slots = arrived_ref.shape[0]
    meta = arrived_ref[:, model:].astype(f32)
    slot_column = jnp.where(
        meta[:, 3 * heads + 1 : 3 * heads + 2] > 0.5, meta[:, 3 * heads : 3 * heads + 1], -1.0
    )
    slot_wide = jnp.broadcast_to(slot_column, (slots, lanes))
    for image in range(count):
        peak_ref[image : image + 1, :] = jnp.max(
            jnp.where(slot_wide == float(image), meta, very_low), axis=0, keepdims=True
        )
    base_peak = base_peak_ref[...]
    joint = jnp.maximum(peak_ref[...], base_peak)
    member = (slot_column == iota((slots, count), 1).astype(f32)).astype(f32)
    joint_at = jnp.dot(member, joint, preferred_element_type=f32, precision=highest)
    used = (iota((slots, lanes), 1) < heads) & (slot_wide >= 0.0)
    rescale = jnp.where(used, jnp.exp(jnp.where(used, meta - joint_at, 0.0)), 0.0).astype(bf16)
    totals = jnp.roll(meta, -heads, axis=1) + jnp.roll(meta, -2 * heads, axis=1)
    lane = iota((count, lanes), 1)
    base_rescale = jnp.where(lane < heads, jnp.exp(base_peak - joint), 0.0)
    collected = lax.dot_general(
        member,
        totals * rescale.astype(f32),
        (((0,), (0,)), ((), ())),
        preferred_element_type=f32,
        precision=highest,
    )
    inverse = 1.0 / (collected + base_total_ref[...] * base_rescale + jnp.where(lane < heads, 0.0, 1.0))
    table_shape = (lanes, model)
    table_row = iota(table_shape, 0)
    column = iota(table_shape, 1) - head_lane(table_row, heads, per_tile) * head_dim
    table = ((column >= 0) & (column < head_dim) & (table_row < heads)).astype(bf16)
    scaled = arrived_ref[:, :model].astype(f32) * jnp.dot(
        rescale, table, preferred_element_type=f32
    )
    crop_sum = lax.dot_general(
        member.astype(bf16),
        scaled.astype(bf16),
        (((0,), (0,)), ((), ())),
        preferred_element_type=f32,
    )
    factors = two_part_dot(jnp.concatenate([inverse, base_rescale * inverse], axis=0), table)
    pooled = (crop_sum * factors[:count] + base_ref[...] * factors[count:]).astype(bf16)
    text = text_ref[...].astype(f32)
    text_unit = (
        text * lax.rsqrt(jnp.sum(text * text, axis=1, keepdims=True) + norm_eps)
    ).astype(bf16)
    double = 2 * count
    for part in range(model // lanes):
        own_ref[part * double + count : (part + 1) * double, :] = text_unit[
            :, part * lanes : (part + 1) * lanes
        ]
    own_ref[model // lanes * double :, :] = jnp.broadcast_to(
        jnp.concatenate([label_ref[...].astype(f32)] * (lanes // count), axis=1),
        (own_ref.shape[0] - model // lanes * double, lanes),
    ).astype(bf16)
    features = jnp.dot(pooled, out_weight_ref[...], preferred_element_type=f32)
    embed_ref[...] = features.astype(bf16)
    image_unit = (
        features * lax.rsqrt(jnp.sum(features * features, axis=1, keepdims=True) + norm_eps)
    ).astype(bf16)
    for part in range(model // lanes):
        own_ref[part * double : part * double + count, :] = image_unit[
            :, part * lanes : (part + 1) * lanes
        ]


def grad_kernel(scale_ref, bias_ref, label_ref, *refs):
    pieces, (image_grad_ref, text_grad_ref, everyone) = refs[:-3], refs[-3:]
    count, model = image_grad_ref.shape
    double = 2 * count
    parts = model // lanes
    label_rows = []
    for index, piece in enumerate(pieces):
        for part in range(parts):
            everyone[
                index * double : (index + 1) * double, part * lanes : (part + 1) * lanes
            ] = piece[part * double : (part + 1) * double, :]
        label_rows.append(piece[parts * double :, :].astype(f32)[:1])
    lane = iota((1, lanes), 1)
    per_row = lanes // double
    label_row = []
    for first in range(0, len(pieces), per_row):
        row = label_rows[first]
        for k in range(1, per_row):
            row = jnp.where(lane >= k * double, label_rows[first + k], row)
        label_row.append(row)
    label_row = jnp.concatenate(label_row, axis=1)
    label_column = column_of(label_ref[...]).astype(f32)
    label_column = jnp.concatenate([label_column, label_column], axis=0)
    scale = scale_ref[0]
    bias = bias_ref[0]
    sign = jnp.where(label_column == label_row, 1.0, -1.0)
    logits = scale * lax.dot_general(
        everyone[:double, :], everyone[...], contract_last, preferred_element_type=f32
    ) + bias
    tile = scale * (-sign * jax.nn.sigmoid(-sign * logits))
    other_side = (iota(tile.shape, 1) % double >= count) == (iota(tile.shape, 0) < count)
    tile = jnp.where(other_side, tile, 0.0).astype(bf16)
    grads = jnp.dot(tile, everyone[...], preferred_element_type=f32)
    image_grad_ref[...] = grads[:count]
    text_grad_ref[...] = grads[count:]


def per_device(
    crop_tokens,
    crop_lengths,
    crop_owner,
    crop_slot,
    base_tokens,
    key_probe,
    value_weight,
    out_weight,
    text_embed,
    pair_labels,
    logit_scale,
    logit_bias,
):
    owners = lax.axis_size("dp")
    peers = lax.axis_size("loop")
    crops, width, model = crop_tokens.shape
    count, base_width, _ = base_tokens.shape
    heads = key_probe.shape[1]
    capacity = max(2, (2 * crops + owners - 1) // owners)
    slots = owners * capacity
    padded = model + lanes
    blocks = 8
    per_tile = sublanes * width // token_tile
    rows = crops * per_tile
    payload = (model // lanes * 2 * count + 16, lanes)
    vmem = pl.BlockSpec(memory_space=pltpu.VMEM)
    smem = pl.BlockSpec(memory_space=pltpu.SMEM)
    anywhere = pl.BlockSpec(memory_space=pl.ANY)
    probe_rows = key_probe.T

    def crop_body(*refs):
        crop_kernel(*refs, capacity=capacity)

    def base_body(*refs):
        base_kernel(*refs, per_tile=per_tile)

    def merge_body(*refs):
        merge_kernel(*refs, heads=heads, per_tile=per_tile)

    send = pl.pallas_call(
        crop_body,
        in_specs=[anywhere, vmem, vmem, vmem, vmem, anywhere],
        out_specs=vmem,
        scratch_shapes=[
            pltpu.VMEM((crops, width, model), bf16),
            pltpu.VMEM((crops * heads, model), bf16),
            pltpu.VMEM((rows, lanes), f32),
            pltpu.VMEM((rows, lanes), jnp.int32),
            pltpu.VMEM((slots, rows), bf16),
            pltpu.VMEM((model, model), bf16),
            pltpu.SemaphoreType.DMA((blocks,)),
            pltpu.SemaphoreType.DMA,
        ],
        out_shape=jax.ShapeDtypeStruct((slots, padded), bf16),
        name="crop_partial",
    )(
        crop_tokens,
        probe_rows,
        crop_lengths,
        crop_owner.reshape(1, crops),
        crop_slot.reshape(1, crops),
        value_weight,
    )
    arrived = lax.all_to_all(send, "dp", split_axis=0, concat_axis=0, tiled=True)
    arrived = pltpu.with_memory_space_constraint(arrived, pltpu.VMEM)
    base_sum, base_peak, base_total = pl.pallas_call(
        base_body,
        in_specs=[anywhere, vmem, anywhere],
        out_specs=[vmem] * 3,
        out_shape=[
            jax.ShapeDtypeStruct((count, model), f32),
            jax.ShapeDtypeStruct((count, lanes), f32),
            jax.ShapeDtypeStruct((count, lanes), f32),
        ],
        scratch_shapes=[
            pltpu.VMEM((count, base_width, model), bf16),
            pltpu.VMEM((count * heads, model), bf16),
            pltpu.VMEM((model, model), bf16),
            pltpu.SemaphoreType.DMA((count * base_width // token_tile,)),
            pltpu.SemaphoreType.DMA,
        ],
        name="base_partial",
    )(base_tokens, probe_rows, value_weight)
    label_row = pair_labels.reshape(1, count)
    image_embed, own = pl.pallas_call(
        merge_body,
        in_specs=[vmem] * 7,
        out_specs=[vmem] * 2,
        out_shape=[
            jax.ShapeDtypeStruct((count, model), bf16),
            jax.ShapeDtypeStruct(payload, bf16),
        ],
        scratch_shapes=[pltpu.VMEM((count, lanes), f32)],
        name="merge_parts",
    )(
        arrived,
        base_sum,
        base_peak,
        base_total,
        text_embed,
        label_row,
        pltpu.with_memory_space_constraint(out_weight, pltpu.VMEM),
    )

    def peer_copy(array, half, turn):
        column = peers // 2
        pairs = [
            (p, (p // column ^ half) * column + (p % column + turn) % column) for p in range(peers)
        ]
        return lax.ppermute(array, "loop", pairs)

    other = peer_copy(own, 1, 0)
    across = peer_copy(own, 0, 2)
    after = peer_copy(own, 0, 1)
    before = peer_copy(own, 0, 3)
    received = [
        other,
        after,
        before,
        across,
        peer_copy(other, 0, 1),
        peer_copy(other, 0, 3),
        peer_copy(across, 1, 0),
    ]
    pieces = [own] + [pltpu.with_memory_space_constraint(piece, pltpu.VMEM) for piece in received]
    image_grad, text_grad = pl.pallas_call(
        grad_kernel,
        in_specs=[smem, smem, vmem] + [vmem] * peers,
        out_specs=[vmem] * 2,
        out_shape=[
            jax.ShapeDtypeStruct((count, model), f32),
            jax.ShapeDtypeStruct((count, model), f32),
        ],
        scratch_shapes=[pltpu.VMEM((peers * 2 * count, model), bf16)],
        name="loss_grads",
    )(logit_scale, logit_bias, label_row, *pieces)
    return (image_embed, image_grad, text_grad)


def solution(mesh):
    return jax.shard_map(
        per_device,
        mesh=mesh,
        in_specs=(
            P(("dp", "loop"), None, None),
            P(("dp", "loop"), None),
            P(("dp", "loop"), None),
            P(("dp", "loop")),
            P(("dp", "loop"), None, None),
            P(),
            P(),
            P(),
            P(("dp", "loop"), None),
            P(("dp", "loop")),
            P(),
            P(),
        ),
        out_specs=(P(("dp", "loop"), None), P(("dp", "loop"), None), P(("dp", "loop"), None)),
        check_vma=False,
    )
```

```python
import math

import jax
import jax.numpy as jnp
from jax import lax
from jax.experimental import pallas as pl
from jax.experimental.pallas import tpu as pltpu
from jax.sharding import PartitionSpec as P

very_low = -1e30
norm_eps = 1e-06
highest = lax.Precision.HIGHEST
f32 = jnp.float32
bf16 = jnp.bfloat16
contract_last = (((1,), (1,)), ((), ()))
lanes = 128
sublanes = 8
col_tile = 256
token_tile = 256


def iota(shape, dim):
    return lax.broadcasted_iota(jnp.int32, shape, dim)


def head_lane(lane, heads, per_tile):
    return (lane % (heads // per_tile)) * per_tile + lane // (heads // per_tile)


def score_rows(probe_rows, tokens, head_dim):
    return lax.dot_general(
        probe_rows, tokens, contract_last, preferred_element_type=f32
    ) * (1.0 / math.sqrt(head_dim))


def softmax_rows(scores, valid, units, rounded):
    heads = scores.shape[0]
    per_tile = sublanes // units
    tiles = heads // per_tile
    row = iota(valid.shape, 0)
    lane = iota((sublanes, lanes), 1)
    peaks = jnp.zeros((sublanes, lanes), f32)
    totals = jnp.zeros((sublanes, lanes), f32)
    weights = []
    for tile in range(tiles):
        part = jnp.broadcast_to(scores[tile * per_tile : tile * per_tile + 1, :], valid.shape)
        for k in range(1, per_tile):
            head = tile * per_tile + k
            part = jnp.where(row >= k * units, scores[head : head + 1, :], part)
        masked = jnp.where(valid, part, very_low)
        peak = jnp.max(masked, axis=1, keepdims=True)
        if rounded:
            peak = peak.astype(bf16).astype(f32)
        weight = jnp.exp(masked - peak).astype(bf16).astype(f32)
        amount = jnp.sum(weight, axis=1, keepdims=True)
        peaks = jnp.where(lane == tile, peak, peaks)
        totals = jnp.where(lane == tile, amount, totals)
        weights.append(weight)
    row = iota((sublanes, lanes), 0)
    for k in range(1, per_tile):
        peaks = jnp.where(row >= k * units, jnp.roll(peaks, k * tiles, axis=1), peaks)
        totals = jnp.where(row >= k * units, jnp.roll(totals, k * tiles, axis=1), totals)
    return jnp.concatenate(weights, axis=0).astype(bf16), peaks, totals


def mix_rows(rows_ref, stride, step, weights, tokens):
    mixed = [
        jnp.dot(weight, token, preferred_element_type=f32)
        for weight, token in zip(weights, tokens)
    ]
    height = len(mixed) * sublanes
    for tile in range(mixed[0].shape[0] // sublanes):
        start = tile * stride + step * height
        if not isinstance(start, int):
            start = pl.multiple_of(start, height)
        rows_ref[pl.ds(start, height), :] = jnp.concatenate(
            [part[tile * sublanes : (tile + 1) * sublanes, :] for part in mixed], axis=0
        ).astype(bf16)


def project_tile(rows_ref, value_ref, stride, low, high, head_dim, units):
    span = sublanes // units * head_dim
    first = low // span
    last = (high - 1) // span
    stacked = jnp.dot(
        rows_ref[first * stride : (last + 1) * stride, :],
        value_ref[:, low:high],
        preferred_element_type=f32,
    ).reshape(last + 1 - first, stride // sublanes, sublanes, high - low)
    shape = (1, sublanes, high - low)
    kind = iota(shape, 1) // units
    column = iota(shape, 2) + low - kind * head_dim
    total = jnp.where(column >= first * span, stacked[0], 0.0)
    for tile in range(first + 1, last + 1):
        total = jnp.where(column >= tile * span, stacked[tile - first], total)
    if units < sublanes:
        owner = (column >= 0) & (column % span < head_dim)
        total = jnp.where(owner, total, 0.0)
    return total.reshape(stride, high - low)


def project_heads(rows_ref, value_ref, stride, model, head_dim, units, finish):
    waiting = None
    for low in range(0, model, col_tile):
        high = min(low + col_tile, model)
        current = project_tile(rows_ref, value_ref, stride, low, high, head_dim, units)
        if waiting is not None:
            finish(*waiting)
        waiting = (low, high, current)
    finish(*waiting)


def column_of(row):
    square = (row.shape[1], row.shape[1])
    return jnp.sum(jnp.where(iota(square, 0) == iota(square, 1), row, 0), axis=1, keepdims=True)


def crop_kernel(
    token_hbm,
    probe_ref,
    length_ref,
    owner_ref,
    slot_ref,
    value_hbm,
    send_ref,
    token_ref,
    rows_ref,
    meta_ref,
    limit_ref,
    member_ref,
    value_ref,
    token_sem,
    value_sem,
    *,
    capacity,
):
    crops, width, model = token_ref.shape
    heads = probe_ref.shape[0]
    head_dim = model // heads
    slots = send_ref.shape[0]
    units = token_tile // width
    per_tile = sublanes // units
    rows = crops * per_tile
    blocks = token_sem.shape[0]
    per_step = crops // blocks
    parts = per_step // units

    def token_copy(step):
        where = pl.ds(step * per_step, per_step)
        return pltpu.make_async_copy(token_hbm.at[where], token_ref.at[where], token_sem.at[step])

    for step in range(blocks):
        token_copy(step).start()
    value_copy = pltpu.make_async_copy(value_hbm, value_ref, value_sem)
    value_copy.start()
    expand = (rows, crops)
    owner_of = iota(expand, 0) // sublanes * units + iota(expand, 0) % units
    chosen = owner_of == iota(expand, 1)
    limit_ref[...] = jnp.broadcast_to(
        jnp.sum(jnp.where(chosen, length_ref[...], 0), axis=1, keepdims=True), limit_ref.shape
    )
    wide = (sublanes, token_tile)
    offset = iota(wide, 1) - iota(wide, 0) % units * width

    def tokens_of(step, part):
        start = step * per_step + part * units
        return token_ref[pl.ds(start, units)].reshape(units * width, model)

    owner_row = owner_ref[...]
    square = (crops, crops)
    earlier = (column_of(owner_row) == owner_row) & (iota(square, 0) < iota(square, 1))
    rank = jnp.sum(earlier.astype(jnp.int32), axis=0, keepdims=True)
    place = owner_row * capacity + rank
    turned = (crops, rows)
    place_row = jnp.sum(
        jnp.where(
            iota(turned, 1) // sublanes * units + iota(turned, 1) % units == iota(turned, 0),
            column_of(place),
            0,
        ),
        axis=0,
        keepdims=True,
    )
    member_ref[...] = (iota((slots, rows), 0) == place_row).astype(bf16)
    slot_of = jnp.sum(jnp.where(chosen, slot_ref[...], 0), axis=1, keepdims=True)
    lane = iota((rows, lanes), 1)
    lead = iota((rows, lanes), 0) % sublanes < units
    extra = jnp.where(lane == 3 * heads, slot_of.astype(f32), 0.0) + jnp.where(
        lane == 3 * heads + 1, 1.0, 0.0
    )
    meta_ref[...] = jnp.where(lead, extra, 0.0)

    def scores_of(step):
        return tuple(
            score_rows(probe_ref[...], tokens_of(step, part), head_dim) for part in range(parts)
        )

    def weigh(step, scores):
        weights = []
        for part in range(parts):
            start = pl.multiple_of((step * parts + part) * sublanes, sublanes)
            limit = jnp.concatenate(
                [limit_ref[pl.ds(start, sublanes), :]] * (token_tile // lanes), axis=1
            )
            weight, peaks, totals = softmax_rows(
                scores[part], (offset >= 0) & (offset < limit), units, True
            )
            coarse = totals.astype(bf16).astype(f32)
            meta_ref[pl.ds(start, sublanes), :] += (
                peaks
                + jnp.roll(coarse, heads, axis=1)
                + jnp.roll(totals - coarse, 2 * heads, axis=1)
            )
            weights.append(weight)
        return tuple(weights)

    def mix(step, weights):
        mix_rows(
            rows_ref, rows, step, weights, [tokens_of(step, part) for part in range(parts)]
        )

    token_copy(0).wait()
    scores = scores_of(0)
    token_copy(1).wait()
    following = scores_of(1)
    weights = weigh(0, scores)

    def advance(step, carry):
        scores, weights = carry
        token_copy(step + 1).wait()
        mix(step - 1, weights)
        following = scores_of(step + 1)
        return following, weigh(step, scores)

    scores, weights = lax.fori_loop(1, blocks - 1, advance, (following, weights))
    mix(blocks - 2, weights)
    mix(blocks - 1, weigh(blocks - 1, scores))
    send_ref[:, model:] = jnp.dot(
        member_ref[...], meta_ref[...].astype(bf16), preferred_element_type=f32
    ).astype(bf16)
    value_copy.wait()

    def finish(low, high, summed):
        send_ref[:, low:high] = jnp.dot(
            member_ref[...], summed.astype(bf16), preferred_element_type=f32
        ).astype(bf16)

    project_heads(rows_ref, value_ref, rows, model, head_dim, units, finish)


def base_kernel(
    token_hbm,
    probe_ref,
    value_hbm,
    sum_ref,
    peak_ref,
    total_ref,
    token_ref,
    rows_ref,
    value_ref,
    token_sem,
    value_sem,
    *,
    per_tile,
):
    count, width, model = token_ref.shape
    heads = probe_ref.shape[0]
    head_dim = model // heads
    units = token_tile // width
    blocks = count // units
    copies = []
    for block in range(blocks):
        where = pl.ds(block * units, units)
        copies.append(
            pltpu.make_async_copy(token_hbm.at[where], token_ref.at[where], token_sem.at[block])
        )
        copies[-1].start()
    value_copy = pltpu.make_async_copy(value_hbm, value_ref, value_sem)
    value_copy.start()
    wide = (sublanes, token_tile)
    offset = iota(wide, 1) - iota(wide, 0) * width
    valid = (offset >= 0) & (offset < width)
    lane = iota((lanes, lanes), 1)
    order = (head_lane(lane, heads, per_tile) == iota((lanes, lanes), 0)) & (lane < heads)
    stats = []
    weights = []
    tokens = []
    for block in range(blocks):
        copies[block].wait()
        tokens.append(
            token_ref[block * units : (block + 1) * units].reshape(units * width, model)
        )
        scores = score_rows(probe_ref[...], tokens[block], head_dim)
        weight, peaks, totals = softmax_rows(scores, valid, units, False)
        weights.append(weight)
        stats.append((peaks, totals))
        if block % 2 == 1:
            pair = slice(block - 1, block + 1)
            mix_rows(rows_ref, count, block // 2, weights[pair], tokens[pair])
    for index, out_ref in ((0, peak_ref), (1, total_ref)):
        out_ref[...] = jnp.dot(
            jnp.concatenate([pair[index] for pair in stats], axis=0),
            order.astype(f32),
            preferred_element_type=f32,
            precision=highest,
        )
    value_copy.wait()

    def finish(low, high, summed):
        sum_ref[:, low:high] = summed

    project_heads(rows_ref, value_ref, count, model, head_dim, units, finish)


def two_part_dot(matrix, table):
    coarse = matrix.astype(bf16)
    fine = (matrix - coarse.astype(f32)).astype(bf16)
    return jnp.dot(coarse, table, preferred_element_type=f32) + jnp.dot(
        fine, table, preferred_element_type=f32
    )


def merge_kernel(
    arrived_ref,
    base_ref,
    base_peak_ref,
    base_total_ref,
    text_ref,
    label_ref,
    out_weight_ref,
    embed_ref,
    own_ref,
    peak_ref,
    *,
    heads,
    per_tile,
):
    count, model = base_ref.shape
    head_dim = model // heads
    slots = arrived_ref.shape[0]
    meta = arrived_ref[:, model:].astype(f32)
    slot_column = jnp.where(
        meta[:, 3 * heads + 1 : 3 * heads + 2] > 0.5, meta[:, 3 * heads : 3 * heads + 1], -1.0
    )
    slot_wide = jnp.broadcast_to(slot_column, (slots, lanes))
    for image in range(count):
        peak_ref[image : image + 1, :] = jnp.max(
            jnp.where(slot_wide == float(image), meta, very_low), axis=0, keepdims=True
        )
    base_peak = base_peak_ref[...]
    joint = jnp.maximum(peak_ref[...], base_peak)
    member = (slot_column == iota((slots, count), 1).astype(f32)).astype(f32)
    joint_at = jnp.dot(member, joint, preferred_element_type=f32, precision=highest)
    used = (iota((slots, lanes), 1) < heads) & (slot_wide >= 0.0)
    rescale = jnp.where(used, jnp.exp(jnp.where(used, meta - joint_at, 0.0)), 0.0).astype(bf16)
    totals = jnp.roll(meta, -heads, axis=1) + jnp.roll(meta, -2 * heads, axis=1)
    lane = iota((count, lanes), 1)
    base_rescale = jnp.where(lane < heads, jnp.exp(base_peak - joint), 0.0)
    collected = lax.dot_general(
        member,
        totals * rescale.astype(f32),
        (((0,), (0,)), ((), ())),
        preferred_element_type=f32,
        precision=highest,
    )
    inverse = 1.0 / (collected + base_total_ref[...] * base_rescale + jnp.where(lane < heads, 0.0, 1.0))
    table_shape = (lanes, model)
    table_row = iota(table_shape, 0)
    column = iota(table_shape, 1) - head_lane(table_row, heads, per_tile) * head_dim
    table = ((column >= 0) & (column < head_dim) & (table_row < heads)).astype(bf16)
    scaled = arrived_ref[:, :model].astype(f32) * jnp.dot(
        rescale, table, preferred_element_type=f32
    )
    crop_sum = lax.dot_general(
        member.astype(bf16),
        scaled.astype(bf16),
        (((0,), (0,)), ((), ())),
        preferred_element_type=f32,
    )
    factors = two_part_dot(jnp.concatenate([inverse, base_rescale * inverse], axis=0), table)
    pooled = (crop_sum * factors[:count] + base_ref[...] * factors[count:]).astype(bf16)
    text = text_ref[...].astype(f32)
    text_unit = (
        text * lax.rsqrt(jnp.sum(text * text, axis=1, keepdims=True) + norm_eps)
    ).astype(bf16)
    double = 2 * count
    for part in range(model // lanes):
        own_ref[part * double + count : (part + 1) * double, :] = text_unit[
            :, part * lanes : (part + 1) * lanes
        ]
    own_ref[model // lanes * double :, :] = jnp.broadcast_to(
        jnp.concatenate([label_ref[...].astype(f32)] * (lanes // count), axis=1),
        (own_ref.shape[0] - model // lanes * double, lanes),
    ).astype(bf16)
    features = jnp.dot(pooled, out_weight_ref[...], preferred_element_type=f32)
    embed_ref[...] = features.astype(bf16)
    image_unit = (
        features * lax.rsqrt(jnp.sum(features * features, axis=1, keepdims=True) + norm_eps)
    ).astype(bf16)
    for part in range(model // lanes):
        own_ref[part * double : part * double + count, :] = image_unit[
            :, part * lanes : (part + 1) * lanes
        ]


def grad_kernel(scale_ref, bias_ref, label_ref, *refs):
    pieces, (image_grad_ref, text_grad_ref, everyone) = refs[:-3], refs[-3:]
    count, model = image_grad_ref.shape
    double = 2 * count
    parts = model // lanes
    label_rows = []
    for index, piece in enumerate(pieces):
        for part in range(parts):
            everyone[
                index * double : (index + 1) * double, part * lanes : (part + 1) * lanes
            ] = piece[part * double : (part + 1) * double, :]
        label_rows.append(piece[parts * double :, :].astype(f32)[:1])
    lane = iota((1, lanes), 1)
    per_row = lanes // double
    label_row = []
    for first in range(0, len(pieces), per_row):
        row = label_rows[first]
        for k in range(1, per_row):
            row = jnp.where(lane >= k * double, label_rows[first + k], row)
        label_row.append(row)
    label_row = jnp.concatenate(label_row, axis=1)
    label_column = column_of(label_ref[...]).astype(f32)
    label_column = jnp.concatenate([label_column, label_column], axis=0)
    scale = scale_ref[0]
    bias = bias_ref[0]
    sign = jnp.where(label_column == label_row, 1.0, -1.0)
    logits = scale * lax.dot_general(
        everyone[:double, :], everyone[...], contract_last, preferred_element_type=f32
    ) + bias
    tile = scale * (-sign * jax.nn.sigmoid(-sign * logits))
    other_side = (iota(tile.shape, 1) % double >= count) == (iota(tile.shape, 0) < count)
    tile = jnp.where(other_side, tile, 0.0).astype(bf16)
    grads = jnp.dot(tile, everyone[...], preferred_element_type=f32)
    image_grad_ref[...] = grads[:count]
    text_grad_ref[...] = grads[count:]


def per_device(
    crop_tokens,
    crop_lengths,
    crop_owner,
    crop_slot,
    base_tokens,
    key_probe,
    value_weight,
    out_weight,
    text_embed,
    pair_labels,
    logit_scale,
    logit_bias,
):
    owners = lax.axis_size("dp")
    peers = lax.axis_size("loop")
    crops, width, model = crop_tokens.shape
    count, base_width, _ = base_tokens.shape
    heads = key_probe.shape[1]
    capacity = max(2, (2 * crops + owners - 1) // owners)
    slots = owners * capacity
    padded = model + lanes
    blocks = 8
    per_tile = sublanes * width // token_tile
    rows = crops * per_tile
    payload = (model // lanes * 2 * count + 16, lanes)
    vmem = pl.BlockSpec(memory_space=pltpu.VMEM)
    smem = pl.BlockSpec(memory_space=pltpu.SMEM)
    anywhere = pl.BlockSpec(memory_space=pl.ANY)
    probe_rows = key_probe.T

    def crop_body(*refs):
        crop_kernel(*refs, capacity=capacity)

    def base_body(*refs):
        base_kernel(*refs, per_tile=per_tile)

    def merge_body(*refs):
        merge_kernel(*refs, heads=heads, per_tile=per_tile)

    send = pl.pallas_call(
        crop_body,
        in_specs=[anywhere, vmem, vmem, vmem, vmem, anywhere],
        out_specs=vmem,
        scratch_shapes=[
            pltpu.VMEM((crops, width, model), bf16),
            pltpu.VMEM((crops * heads, model), bf16),
            pltpu.VMEM((rows, lanes), f32),
            pltpu.VMEM((rows, lanes), jnp.int32),
            pltpu.VMEM((slots, rows), bf16),
            pltpu.VMEM((model, model), bf16),
            pltpu.SemaphoreType.DMA((blocks,)),
            pltpu.SemaphoreType.DMA,
        ],
        out_shape=jax.ShapeDtypeStruct((slots, padded), bf16),
        name="crop_partial",
    )(
        crop_tokens,
        probe_rows,
        crop_lengths,
        crop_owner.reshape(1, crops),
        crop_slot.reshape(1, crops),
        value_weight,
    )
    arrived = lax.all_to_all(send, "dp", split_axis=0, concat_axis=0, tiled=True)
    arrived = pltpu.with_memory_space_constraint(arrived, pltpu.VMEM)
    base_sum, base_peak, base_total = pl.pallas_call(
        base_body,
        in_specs=[anywhere, vmem, anywhere],
        out_specs=[vmem] * 3,
        out_shape=[
            pltpu.VMEM((count, model), f32),
            pltpu.VMEM((count, lanes), f32),
            pltpu.VMEM((count, lanes), f32),
        ],
        scratch_shapes=[
            pltpu.VMEM((count, base_width, model), bf16),
            pltpu.VMEM((count * heads, model), bf16),
            pltpu.VMEM((model, model), bf16),
            pltpu.SemaphoreType.DMA((count * base_width // token_tile,)),
            pltpu.SemaphoreType.DMA,
        ],
        name="base_partial",
    )(base_tokens, probe_rows, value_weight)
    label_row = pltpu.with_memory_space_constraint(pair_labels.reshape(1, count), pltpu.VMEM)
    image_embed, own = pl.pallas_call(
        merge_body,
        in_specs=[vmem] * 7,
        out_specs=[vmem] * 2,
        out_shape=[
            pltpu.VMEM((count, model), bf16),
            pltpu.VMEM(payload, bf16),
        ],
        scratch_shapes=[pltpu.VMEM((count, lanes), f32)],
        name="merge_parts",
    )(
        arrived,
        pltpu.with_memory_space_constraint(base_sum, pltpu.VMEM),
        pltpu.with_memory_space_constraint(base_peak, pltpu.VMEM),
        pltpu.with_memory_space_constraint(base_total, pltpu.VMEM),
        pltpu.with_memory_space_constraint(text_embed, pltpu.VMEM),
        label_row,
        pltpu.with_memory_space_constraint(out_weight, pltpu.VMEM),
    )

    def peer_copy(array, half, turn):
        column = peers // 2
        pairs = [
            (p, (p // column ^ half) * column + (p % column + turn) % column) for p in range(peers)
        ]
        return lax.ppermute(array, "loop", pairs)

    other = peer_copy(own, 1, 0)
    across = peer_copy(own, 0, 2)
    after = peer_copy(own, 0, 1)
    before = peer_copy(own, 0, 3)
    received = [
        other,
        after,
        before,
        across,
        peer_copy(other, 0, 1),
        peer_copy(other, 0, 3),
        peer_copy(across, 1, 0),
    ]
    pieces = [pltpu.with_memory_space_constraint(piece, pltpu.VMEM) for piece in [own] + received]
    image_grad, text_grad = pl.pallas_call(
        grad_kernel,
        in_specs=[smem, smem, vmem] + [vmem] * peers,
        out_specs=[vmem] * 2,
        out_shape=[
            jax.ShapeDtypeStruct((count, model), f32),
            jax.ShapeDtypeStruct((count, model), f32),
        ],
        scratch_shapes=[pltpu.VMEM((peers * 2 * count, model), bf16)],
        name="loss_grads",
    )(logit_scale, logit_bias, label_row, *pieces)
    return (image_embed, image_grad, text_grad)


def solution(mesh):
    return jax.shard_map(
        per_device,
        mesh=mesh,
        in_specs=(
            P(("dp", "loop"), None, None),
            P(("dp", "loop"), None),
            P(("dp", "loop"), None),
            P(("dp", "loop")),
            P(("dp", "loop"), None, None),
            P(),
            P(),
            P(),
            P(("dp", "loop"), None),
            P(("dp", "loop")),
            P(),
            P(),
        ),
        out_specs=(P(("dp", "loop"), None), P(("dp", "loop"), None), P(("dp", "loop"), None)),
        check_vma=False,
    )
```

```python
import math

import jax
import jax.numpy as jnp
from jax import lax
from jax.experimental import pallas as pl
from jax.experimental.pallas import tpu as pltpu
from jax.sharding import PartitionSpec as P

very_low = -1e30
norm_eps = 1e-06
highest = lax.Precision.HIGHEST
f32 = jnp.float32
bf16 = jnp.bfloat16
contract_last = (((1,), (1,)), ((), ()))
lanes = 128
sublanes = 8
col_tile = 256
token_tile = 256


def iota(shape, dim):
    return lax.broadcasted_iota(jnp.int32, shape, dim)


def head_lane(lane, heads, per_tile):
    return (lane % (heads // per_tile)) * per_tile + lane // (heads // per_tile)


def score_rows(probe_rows, tokens, head_dim):
    return lax.dot_general(
        probe_rows, tokens, contract_last, preferred_element_type=f32
    ) * (1.0 / math.sqrt(head_dim))


def softmax_rows(scores, valid, units, rounded):
    heads = scores.shape[0]
    per_tile = sublanes // units
    tiles = heads // per_tile
    row = iota(valid.shape, 0)
    lane = iota((sublanes, lanes), 1)
    peaks = jnp.zeros((sublanes, lanes), f32)
    totals = jnp.zeros((sublanes, lanes), f32)
    weights = []
    for tile in range(tiles):
        part = jnp.broadcast_to(scores[tile * per_tile : tile * per_tile + 1, :], valid.shape)
        for k in range(1, per_tile):
            head = tile * per_tile + k
            part = jnp.where(row >= k * units, scores[head : head + 1, :], part)
        masked = jnp.where(valid, part, very_low)
        peak = jnp.max(masked, axis=1, keepdims=True)
        if rounded:
            peak = peak.astype(bf16).astype(f32)
        weight = jnp.exp(masked - peak).astype(bf16).astype(f32)
        amount = jnp.sum(weight, axis=1, keepdims=True)
        peaks = jnp.where(lane == tile, peak, peaks)
        totals = jnp.where(lane == tile, amount, totals)
        weights.append(weight)
    row = iota((sublanes, lanes), 0)
    for k in range(1, per_tile):
        peaks = jnp.where(row >= k * units, jnp.roll(peaks, k * tiles, axis=1), peaks)
        totals = jnp.where(row >= k * units, jnp.roll(totals, k * tiles, axis=1), totals)
    return jnp.concatenate(weights, axis=0).astype(bf16), peaks, totals


def mix_rows(rows_ref, stride, step, weights, tokens):
    mixed = [
        jnp.dot(weight, token, preferred_element_type=f32)
        for weight, token in zip(weights, tokens)
    ]
    height = len(mixed) * sublanes
    for tile in range(mixed[0].shape[0] // sublanes):
        start = tile * stride + step * height
        if not isinstance(start, int):
            start = pl.multiple_of(start, height)
        rows_ref[pl.ds(start, height), :] = jnp.concatenate(
            [part[tile * sublanes : (tile + 1) * sublanes, :] for part in mixed], axis=0
        ).astype(bf16)


def project_tile(rows_ref, value_ref, stride, low, high, head_dim, units, begin=0, end=None):
    span = sublanes // units * head_dim
    first = low // span
    last = (high - 1) // span
    end = stride if end is None else end
    stacked = jnp.dot(
        jnp.concatenate(
            [
                rows_ref[tile * stride + begin : tile * stride + end, :]
                for tile in range(first, last + 1)
            ],
            axis=0,
        ),
        value_ref[:, low:high],
        preferred_element_type=f32,
    ).reshape(last + 1 - first, (end - begin) // sublanes, sublanes, high - low)
    shape = (1, sublanes, high - low)
    kind = iota(shape, 1) // units
    column = iota(shape, 2) + low - kind * head_dim
    total = jnp.where(column >= first * span, stacked[0], 0.0)
    for tile in range(first + 1, last + 1):
        total = jnp.where(column >= tile * span, stacked[tile - first], total)
    if units < sublanes:
        owner = (column >= 0) & (column % span < head_dim)
        total = jnp.where(owner, total, 0.0)
    return total.reshape(end - begin, high - low)


def project_heads(rows_ref, value_ref, stride, model, head_dim, units, finish):
    waiting = None
    for low in range(0, model, col_tile):
        high = min(low + col_tile, model)
        current = project_tile(rows_ref, value_ref, stride, low, high, head_dim, units)
        if waiting is not None:
            finish(*waiting)
        waiting = (low, high, current)
    finish(*waiting)


def column_of(row):
    square = (row.shape[1], row.shape[1])
    return jnp.sum(jnp.where(iota(square, 0) == iota(square, 1), row, 0), axis=1, keepdims=True)


def crop_kernel(
    token_hbm,
    probe_ref,
    length_ref,
    owner_ref,
    slot_ref,
    value_hbm,
    send_ref,
    token_ref,
    rows_ref,
    meta_ref,
    limit_ref,
    member_ref,
    summed_ref,
    value_ref,
    token_sem,
    value_sem,
    *,
    capacity,
):
    crops, width, model = token_ref.shape
    heads = probe_ref.shape[0]
    head_dim = model // heads
    slots = send_ref.shape[0]
    units = token_tile // width
    per_tile = sublanes // units
    rows = crops * per_tile
    blocks = token_sem.shape[0]
    per_step = crops // blocks
    parts = per_step // units

    def token_copy(step):
        where = pl.ds(step * per_step, per_step)
        return pltpu.make_async_copy(token_hbm.at[where], token_ref.at[where], token_sem.at[step])

    value_copy = pltpu.make_async_copy(value_hbm, value_ref, value_sem)
    for step in range(blocks):
        if step == blocks // 2:
            value_copy.start()
        token_copy(step).start()
    expand = (rows, crops)
    owner_of = iota(expand, 0) // sublanes * units + iota(expand, 0) % units
    chosen = owner_of == iota(expand, 1)
    limit_ref[...] = jnp.broadcast_to(
        jnp.sum(jnp.where(chosen, length_ref[...], 0), axis=1, keepdims=True), limit_ref.shape
    )
    wide = (sublanes, token_tile)
    offset = iota(wide, 1) - iota(wide, 0) % units * width

    def tokens_of(step, part):
        start = step * per_step + part * units
        return token_ref[pl.ds(start, units)].reshape(units * width, model)

    owner_row = owner_ref[...]
    square = (crops, crops)
    earlier = (column_of(owner_row) == owner_row) & (iota(square, 0) < iota(square, 1))
    rank = jnp.sum(earlier.astype(jnp.int32), axis=0, keepdims=True)
    place = owner_row * capacity + rank
    turned = (crops, rows)
    place_row = jnp.sum(
        jnp.where(
            iota(turned, 1) // sublanes * units + iota(turned, 1) % units == iota(turned, 0),
            column_of(place),
            0,
        ),
        axis=0,
        keepdims=True,
    )
    member_ref[...] = (iota((slots, rows), 0) == place_row).astype(bf16)
    slot_of = jnp.sum(jnp.where(chosen, slot_ref[...], 0), axis=1, keepdims=True)
    lane = iota((rows, lanes), 1)
    lead = iota((rows, lanes), 0) % sublanes < units
    extra = jnp.where(lane == 3 * heads, slot_of.astype(f32), 0.0) + jnp.where(
        lane == 3 * heads + 1, 1.0, 0.0
    )
    meta_ref[...] = jnp.where(lead, extra, 0.0)

    def scores_of(step):
        return tuple(
            score_rows(probe_ref[...], tokens_of(step, part), head_dim) for part in range(parts)
        )

    def weigh(step, scores):
        weights = []
        for part in range(parts):
            start = pl.multiple_of((step * parts + part) * sublanes, sublanes)
            limit = jnp.concatenate(
                [limit_ref[pl.ds(start, sublanes), :]] * (token_tile // lanes), axis=1
            )
            weight, peaks, totals = softmax_rows(
                scores[part], (offset >= 0) & (offset < limit), units, True
            )
            coarse = totals.astype(bf16).astype(f32)
            meta_ref[pl.ds(start, sublanes), :] += (
                peaks
                + jnp.roll(coarse, heads, axis=1)
                + jnp.roll(totals - coarse, 2 * heads, axis=1)
            )
            weights.append(weight)
        return tuple(weights)

    def mix(step, weights):
        mix_rows(
            rows_ref, rows, step, weights, [tokens_of(step, part) for part in range(parts)]
        )

    token_copy(0).wait()
    scores = scores_of(0)
    token_copy(1).wait()
    following = scores_of(1)
    weights = weigh(0, scores)

    def advance(step, carry):
        scores, weights = carry
        token_copy(step + 1).wait()
        mix(step - 1, weights)
        following = scores_of(step + 1)
        return following, weigh(step, scores)

    half = rows // 2
    columns = [(low, min(low + col_tile, model)) for low in range(0, model, col_tile)]

    def project(tiles, begin, end):
        for low, high in tiles:
            summed_ref[begin:end, low:high] = project_tile(
                rows_ref, value_ref, rows, low, high, head_dim, units, begin, end
            ).astype(bf16)

    middle = blocks // 2 + 1
    scores, weights = lax.fori_loop(1, middle, advance, (following, weights))
    value_copy.wait()
    spread = blocks - 1 - middle
    for step in range(middle, blocks - 1):
        scores, weights = advance(step, (scores, weights))
        project(columns[step - middle :: spread + 1], 0, half)
    mix(blocks - 2, weights)
    weights = weigh(blocks - 1, scores)
    project(columns[spread :: spread + 1], 0, half)
    mix(blocks - 1, weights)
    project(columns, half, rows)
    send_ref[:, model:] = jnp.dot(
        member_ref[...], meta_ref[...].astype(bf16), preferred_element_type=f32
    ).astype(bf16)
    send_ref[:, :model] = jnp.dot(
        member_ref[...], summed_ref[...], preferred_element_type=f32
    ).astype(bf16)


def base_kernel(
    token_hbm,
    probe_ref,
    value_hbm,
    sum_ref,
    peak_ref,
    total_ref,
    token_ref,
    rows_ref,
    value_ref,
    token_sem,
    value_sem,
    *,
    per_tile,
):
    count, width, model = token_ref.shape
    heads = probe_ref.shape[0]
    head_dim = model // heads
    units = token_tile // width
    blocks = count // units
    copies = []
    for block in range(blocks):
        where = pl.ds(block * units, units)
        copies.append(
            pltpu.make_async_copy(token_hbm.at[where], token_ref.at[where], token_sem.at[block])
        )
        copies[-1].start()
    value_copy = pltpu.make_async_copy(value_hbm, value_ref, value_sem)
    value_copy.start()
    wide = (sublanes, token_tile)
    offset = iota(wide, 1) - iota(wide, 0) * width
    valid = (offset >= 0) & (offset < width)
    lane = iota((lanes, lanes), 1)
    order = (head_lane(lane, heads, per_tile) == iota((lanes, lanes), 0)) & (lane < heads)
    stats = []
    weights = []
    tokens = []
    for block in range(blocks):
        copies[block].wait()
        tokens.append(
            token_ref[block * units : (block + 1) * units].reshape(units * width, model)
        )
        scores = score_rows(probe_ref[...], tokens[block], head_dim)
        weight, peaks, totals = softmax_rows(scores, valid, units, False)
        weights.append(weight)
        stats.append((peaks, totals))
        if block % 2 == 1:
            pair = slice(block - 1, block + 1)
            mix_rows(rows_ref, count, block // 2, weights[pair], tokens[pair])
    for index, out_ref in ((0, peak_ref), (1, total_ref)):
        out_ref[...] = jnp.dot(
            jnp.concatenate([pair[index] for pair in stats], axis=0),
            order.astype(f32),
            preferred_element_type=f32,
            precision=highest,
        )
    value_copy.wait()

    def finish(low, high, summed):
        sum_ref[:, low:high] = summed

    project_heads(rows_ref, value_ref, count, model, head_dim, units, finish)


def two_part_dot(matrix, table):
    coarse = matrix.astype(bf16)
    fine = (matrix - coarse.astype(f32)).astype(bf16)
    return jnp.dot(coarse, table, preferred_element_type=f32) + jnp.dot(
        fine, table, preferred_element_type=f32
    )


def merge_kernel(
    arrived_ref,
    base_ref,
    base_peak_ref,
    base_total_ref,
    text_ref,
    label_ref,
    out_weight_ref,
    embed_ref,
    own_ref,
    peak_ref,
    *,
    heads,
    per_tile,
):
    count, model = base_ref.shape
    head_dim = model // heads
    slots = arrived_ref.shape[0]
    meta = arrived_ref[:, model:].astype(f32)
    slot_column = jnp.where(
        meta[:, 3 * heads + 1 : 3 * heads + 2] > 0.5, meta[:, 3 * heads : 3 * heads + 1], -1.0
    )
    slot_wide = jnp.broadcast_to(slot_column, (slots, lanes))
    for image in range(count):
        peak_ref[image : image + 1, :] = jnp.max(
            jnp.where(slot_wide == float(image), meta, very_low), axis=0, keepdims=True
        )
    base_peak = base_peak_ref[...]
    joint = jnp.maximum(peak_ref[...], base_peak)
    member = (slot_column == iota((slots, count), 1).astype(f32)).astype(f32)
    joint_at = jnp.dot(member, joint, preferred_element_type=f32, precision=highest)
    used = (iota((slots, lanes), 1) < heads) & (slot_wide >= 0.0)
    rescale = jnp.where(used, jnp.exp(jnp.where(used, meta - joint_at, 0.0)), 0.0).astype(bf16)
    totals = jnp.roll(meta, -heads, axis=1) + jnp.roll(meta, -2 * heads, axis=1)
    lane = iota((count, lanes), 1)
    base_rescale = jnp.where(lane < heads, jnp.exp(base_peak - joint), 0.0)
    collected = lax.dot_general(
        member,
        totals * rescale.astype(f32),
        (((0,), (0,)), ((), ())),
        preferred_element_type=f32,
        precision=highest,
    )
    inverse = 1.0 / (collected + base_total_ref[...] * base_rescale + jnp.where(lane < heads, 0.0, 1.0))
    table_shape = (lanes, model)
    table_row = iota(table_shape, 0)
    column = iota(table_shape, 1) - head_lane(table_row, heads, per_tile) * head_dim
    table = ((column >= 0) & (column < head_dim) & (table_row < heads)).astype(bf16)
    scaled = arrived_ref[:, :model].astype(f32) * jnp.dot(
        rescale, table, preferred_element_type=f32
    )
    crop_sum = lax.dot_general(
        member.astype(bf16),
        scaled.astype(bf16),
        (((0,), (0,)), ((), ())),
        preferred_element_type=f32,
    )
    factors = two_part_dot(jnp.concatenate([inverse, base_rescale * inverse], axis=0), table)
    pooled = (crop_sum * factors[:count] + base_ref[...] * factors[count:]).astype(bf16)
    text = text_ref[...].astype(f32)
    text_unit = (
        text * lax.rsqrt(jnp.sum(text * text, axis=1, keepdims=True) + norm_eps)
    ).astype(bf16)
    double = 2 * count
    for part in range(model // lanes):
        own_ref[part * double + count : (part + 1) * double, :] = text_unit[
            :, part * lanes : (part + 1) * lanes
        ]
    own_ref[model // lanes * double :, :] = jnp.broadcast_to(
        jnp.concatenate([label_ref[...].astype(f32)] * (lanes // count), axis=1),
        (own_ref.shape[0] - model // lanes * double, lanes),
    ).astype(bf16)
    features = jnp.dot(pooled, out_weight_ref[...], preferred_element_type=f32)
    embed_ref[...] = features.astype(bf16)
    image_unit = (
        features * lax.rsqrt(jnp.sum(features * features, axis=1, keepdims=True) + norm_eps)
    ).astype(bf16)
    for part in range(model // lanes):
        own_ref[part * double : part * double + count, :] = image_unit[
            :, part * lanes : (part + 1) * lanes
        ]


def grad_kernel(scale_ref, bias_ref, label_ref, *refs):
    pieces, (image_grad_ref, text_grad_ref, everyone) = refs[:-3], refs[-3:]
    count, model = image_grad_ref.shape
    double = 2 * count
    parts = model // lanes
    label_rows = []
    for index, piece in enumerate(pieces):
        for part in range(parts):
            everyone[
                index * double : (index + 1) * double, part * lanes : (part + 1) * lanes
            ] = piece[part * double : (part + 1) * double, :]
        label_rows.append(piece[parts * double :, :].astype(f32)[:1])
    lane = iota((1, lanes), 1)
    per_row = lanes // double
    label_row = []
    for first in range(0, len(pieces), per_row):
        row = label_rows[first]
        for k in range(1, per_row):
            row = jnp.where(lane >= k * double, label_rows[first + k], row)
        label_row.append(row)
    label_row = jnp.concatenate(label_row, axis=1)
    label_column = column_of(label_ref[...]).astype(f32)
    label_column = jnp.concatenate([label_column, label_column], axis=0)
    scale = scale_ref[0]
    bias = bias_ref[0]
    sign = jnp.where(label_column == label_row, 1.0, -1.0)
    logits = scale * lax.dot_general(
        everyone[:double, :], everyone[...], contract_last, preferred_element_type=f32
    ) + bias
    tile = scale * (-sign * jax.nn.sigmoid(-sign * logits))
    other_side = (iota(tile.shape, 1) % double >= count) == (iota(tile.shape, 0) < count)
    tile = jnp.where(other_side, tile, 0.0).astype(bf16)
    grads = jnp.dot(tile, everyone[...], preferred_element_type=f32)
    image_grad_ref[...] = grads[:count]
    text_grad_ref[...] = grads[count:]


def per_device(
    crop_tokens,
    crop_lengths,
    crop_owner,
    crop_slot,
    base_tokens,
    key_probe,
    value_weight,
    out_weight,
    text_embed,
    pair_labels,
    logit_scale,
    logit_bias,
):
    owners = lax.axis_size("dp")
    peers = lax.axis_size("loop")
    crops, width, model = crop_tokens.shape
    count, base_width, _ = base_tokens.shape
    heads = key_probe.shape[1]
    capacity = max(2, (2 * crops + owners - 1) // owners)
    slots = owners * capacity
    padded = model + lanes
    blocks = 8
    per_tile = sublanes * width // token_tile
    rows = crops * per_tile
    payload = (model // lanes * 2 * count + 16, lanes)
    vmem = pl.BlockSpec(memory_space=pltpu.VMEM)
    smem = pl.BlockSpec(memory_space=pltpu.SMEM)
    anywhere = pl.BlockSpec(memory_space=pl.ANY)
    probe_rows = key_probe.T

    def crop_body(*refs):
        crop_kernel(*refs, capacity=capacity)

    def base_body(*refs):
        base_kernel(*refs, per_tile=per_tile)

    def merge_body(*refs):
        merge_kernel(*refs, heads=heads, per_tile=per_tile)

    send = pl.pallas_call(
        crop_body,
        in_specs=[anywhere, vmem, vmem, vmem, vmem, anywhere],
        out_specs=vmem,
        scratch_shapes=[
            pltpu.VMEM((crops, width, model), bf16),
            pltpu.VMEM((crops * heads, model), bf16),
            pltpu.VMEM((rows, lanes), f32),
            pltpu.VMEM((rows, lanes), jnp.int32),
            pltpu.VMEM((slots, rows), bf16),
            pltpu.VMEM((rows, model), bf16),
            pltpu.VMEM((model, model), bf16),
            pltpu.SemaphoreType.DMA((blocks,)),
            pltpu.SemaphoreType.DMA,
        ],
        out_shape=jax.ShapeDtypeStruct((slots, padded), bf16),
        name="crop_partial",
    )(
        crop_tokens,
        probe_rows,
        crop_lengths,
        crop_owner.reshape(1, crops),
        crop_slot.reshape(1, crops),
        value_weight,
    )
    arrived = lax.all_to_all(send, "dp", split_axis=0, concat_axis=0, tiled=True)
    arrived = pltpu.with_memory_space_constraint(arrived, pltpu.VMEM)
    base_sum, base_peak, base_total = pl.pallas_call(
        base_body,
        in_specs=[anywhere, vmem, anywhere],
        out_specs=[vmem] * 3,
        out_shape=[
            pltpu.VMEM((count, model), f32),
            pltpu.VMEM((count, lanes), f32),
            pltpu.VMEM((count, lanes), f32),
        ],
        scratch_shapes=[
            pltpu.VMEM((count, base_width, model), bf16),
            pltpu.VMEM((count * heads, model), bf16),
            pltpu.VMEM((model, model), bf16),
            pltpu.SemaphoreType.DMA((count * base_width // token_tile,)),
            pltpu.SemaphoreType.DMA,
        ],
        name="base_partial",
    )(base_tokens, probe_rows, value_weight)
    label_row = pltpu.with_memory_space_constraint(pair_labels.reshape(1, count), pltpu.VMEM)
    image_embed, own = pl.pallas_call(
        merge_body,
        in_specs=[vmem] * 7,
        out_specs=[vmem] * 2,
        out_shape=[
            pltpu.VMEM((count, model), bf16),
            pltpu.VMEM(payload, bf16),
        ],
        scratch_shapes=[pltpu.VMEM((count, lanes), f32)],
        name="merge_parts",
    )(
        arrived,
        pltpu.with_memory_space_constraint(base_sum, pltpu.VMEM),
        pltpu.with_memory_space_constraint(base_peak, pltpu.VMEM),
        pltpu.with_memory_space_constraint(base_total, pltpu.VMEM),
        pltpu.with_memory_space_constraint(text_embed, pltpu.VMEM),
        label_row,
        pltpu.with_memory_space_constraint(out_weight, pltpu.VMEM),
    )

    def peer_copy(array, half, turn):
        column = peers // 2
        pairs = [
            (p, (p // column ^ half) * column + (p % column + turn) % column) for p in range(peers)
        ]
        return lax.ppermute(array, "loop", pairs)

    other = peer_copy(own, 1, 0)
    across = peer_copy(own, 0, 2)
    after = peer_copy(own, 0, 1)
    before = peer_copy(own, 0, 3)
    received = [
        other,
        after,
        before,
        across,
        peer_copy(other, 0, 1),
        peer_copy(other, 0, 3),
        peer_copy(across, 1, 0),
    ]
    pieces = [pltpu.with_memory_space_constraint(piece, pltpu.VMEM) for piece in [own] + received]
    image_grad, text_grad = pl.pallas_call(
        grad_kernel,
        in_specs=[smem, smem, vmem] + [vmem] * peers,
        out_specs=[vmem] * 2,
        out_shape=[
            jax.ShapeDtypeStruct((count, model), f32),
            jax.ShapeDtypeStruct((count, model), f32),
        ],
        scratch_shapes=[pltpu.VMEM((peers * 2 * count, model), bf16)],
        name="loss_grads",
    )(logit_scale, logit_bias, label_row, *pieces)
    return (image_embed, image_grad, text_grad)


def solution(mesh):
    return jax.shard_map(
        per_device,
        mesh=mesh,
        in_specs=(
            P(("dp", "loop"), None, None),
            P(("dp", "loop"), None),
            P(("dp", "loop"), None),
            P(("dp", "loop")),
            P(("dp", "loop"), None, None),
            P(),
            P(),
            P(),
            P(("dp", "loop"), None),
            P(("dp", "loop")),
            P(),
            P(),
        ),
        out_specs=(P(("dp", "loop"), None), P(("dp", "loop"), None), P(("dp", "loop"), None)),
        check_vma=False,
    )
```
